512 devices in a mesh: section: 16 (over x, y), expert: 32 (over z, core).
Axes of the slice: x: 4, y: 4, z: 16, core: 2. Of those that a mesh axis runs over, the one named last changes fastest.
Arguments:
- x_fwd: bfloat16 [16, 1024, 3584], P('section', 'expert'), may hold values from -6 to 6
- x_bwd: bfloat16 [16, 1024, 3584], P('section', 'expert'), may hold values from -6 to 6
- grad_out: bfloat16 [16, 1024, 3584], P('section', 'expert'), may hold values from -6 to 6
- norm_gain: float32 [16, 3584], P('section'), may hold values from 0.1 to 1.9
- w_gate: bfloat16 [16, 3584, 4096], P('section', None, 'expert'), may hold values from -0.09375 to 0.09375
- w_up: bfloat16 [16, 3584, 4096], P('section', None, 'expert'), may hold values from -0.09375 to 0.09375
- w_down: bfloat16 [16, 4096, 3584], P('section', 'expert'), may hold values from -0.1875 to 0.1875
- route_fwd: int32 [16, 1024, 1], P('section', 'expert'), may hold values from 0 to 3; in each aligned block of 32 rows (0 to 31, 32 to 63, ..., all dimensions but the last counted through in order) at most 12 rows name the same one
- gate_fwd: int32 [16, 1024, 1], P('section', 'expert'), may hold values from 16 to 255
- route_bwd: int32 [16, 1024, 1], P('section', 'expert'), may hold values from 0 to 3; in each aligned block of 32 rows (0 to 31, 32 to 63, ..., all dimensions but the last counted through in order) at most 12 rows name the same one
- gate_bwd: int32 [16, 1024, 1], P('section', 'expert'), may hold values from 16 to 255
Outputs:
- y_next: bfloat16 [16, 1024, 3584], P('section', 'expert')
- dx_prev: bfloat16 [16, 1024, 3584], P('section', 'expert')
The draws below stay inside these ranges and needn't reach their ends.
Inputs may be any that keep to these rules, and one draw needn't show every extreme that they name: `route_fwd`: of one device's 32 tokens of a micro-batch at one section, at most 12 go to one expert, and some expert gets exactly 12 in some such block. `route_bwd`: as for route_fwd.
All inputs are finite; a program needn't handle non-finite values.
Results may differ from the reference program's by a relative error of at most 0.0053.
Values may be sent and summed in bfloat16 or wider, within the bound.
No kernel may reach another device: no remote copies, remote signals or barrier semaphores. Data moves between devices by JAX's collectives and lax.ppermute only.
A program may use at most 64 MiB of HBM per device.

```python
import math
import jax
import jax.numpy as jnp
import numpy as np
from jax import lax

D = 3584
EXP_FF = 1024
EXPERTS = 4
TOK = 32
CAP = 12
SPLIT = 8
HID_DEV = 128
TOKENS = 1024
N_SECTION = 16
N_EXPERT = 32


def plant(values, rng, least, largest):
    spot = [jax.random.randint(jax.random.fold_in(rng, axis), (), 0, length) for axis, length in enumerate(values.shape)]
    widest = values.shape.index(max(values.shape))
    neighbour = spot[:widest] + [(spot[widest] + 1) % values.shape[widest]] + spot[widest + 1:]
    return values.at[tuple(spot)].set(least).at[tuple(neighbour)].set(largest)


def levels(key, extent, shards, least, top_value):
    factor_of, own = 1.0, jax.random.fold_in(key, 6)
    for dim, shards_of in shards:
        draws = jnp.exp(jax.random.uniform(jax.random.fold_in(own, dim), (shards_of,), jnp.float32, least / len(shards), top_value / len(shards)))
        factor_of = factor_of * jnp.repeat(draws, extent[dim] // shards_of).reshape([-1 if axis == dim else 1 for axis in range(len(extent))])
    return factor_of


def assign_block(stream_key, own, number, rows, count, top, reach, skew):
    ranking = jax.random.permutation(stream_key, count)
    crowded, ordinary = load_shares(count, rows * top, reach, skew, True), load_shares(count, rows * top, reach, skew, False)
    places = jnp.arange(count)

    def named(sizes, offset_by):
        used = int((sizes > 0).sum())
        fixed = max(1, used // 4)
        passed = fixed + (places - fixed + offset_by * (used - fixed)) % max(1, count - fixed)
        return jnp.zeros((count,), jnp.int32).at[ranking[jnp.where(places < fixed, places, passed)]].set(jnp.asarray(sizes, jnp.int32))

    sizes = jnp.where(number % 4 == 0, named(crowded, number // 4), named(ordinary, number - number // 4 - 1))
    mixed = jax.random.permutation(jax.random.fold_in(own, 3), count)
    donor, sink = mixed[0:count // 2 * 2:2], mixed[1:count // 2 * 2:2]
    margin = jnp.minimum(sizes[donor] - 1, reach - sizes[sink]) // 2
    margin = jnp.where((donor == ranking[0]) | (sink == ranking[0]) | (sizes[sink] == 0), 0, jnp.maximum(margin, 0))
    passed = jax.random.randint(jax.random.fold_in(own, 4), (count // 2,), 0, 1 << 20) % (margin + 1)
    sizes = sizes.at[donor].add(-passed).at[sink].add(passed)
    members = jnp.searchsorted(jnp.cumsum(sizes), jnp.arange(rows * top), side="right").astype(jnp.int32)
    listing = members.reshape(top, rows).T
    listing = listing[jax.random.permutation(jax.random.fold_in(own, 1), rows)]
    offset_by = jax.random.randint(jax.random.fold_in(own, 2), (rows, 1), 0, top)
    return jnp.take_along_axis(listing, (jnp.arange(top)[None, :] + offset_by) % top, axis=1)


def load_shares(amount, total, reach, lean, full):
    portions = [(1 << 20) // math.isqrt(rank ** lean) + 1 for rank in range(1, amount + 1)]
    largest = reach if full else min(reach, max(-(-total // amount), total * portions[0] // sum(portions)))
    least = 1 if total - largest >= amount - 1 else 0
    given, spare = [largest] + [least] * (amount - 1), total - largest - least * (amount - 1)
    while spare > 0:
        candidates = [i for i in range(1, amount) if given[i] < largest] or [i for i in range(1, amount) if given[i] < reach]
        pool, remaining = sum([portions[i] for i in candidates]), spare
        for i in candidates:
            addition = min(reach - given[i], max(1, remaining * portions[i] // pool), spare)
            given[i] = given[i] + addition
            spare = spare - addition
    return np.array(given)


def bell_draw(rng, extent, spread, limit, split=(), kind=jnp.bfloat16):
    array = jax.random.normal(rng, extent, jnp.float32) * spread
    if len(split) > 0:
        array = levels(rng, extent, split, -0.22, 0.18) * array
    return jnp.clip(array, min=-limit, max=limit).astype(kind)


def setup_inputs(seed: int = 0) -> dict:
    arg_keys = jax.random.split(jax.random.key(seed), 12)
    x_fwd = bell_draw(arg_keys[0], (N_SECTION, TOKENS, D), 1.0, 6.0, ((0, 16), (1, 32)))
    x_bwd = bell_draw(arg_keys[1], (N_SECTION, TOKENS, D), 1.0, 6.0, ((0, 16), (1, 32)))
    grad_out = bell_draw(arg_keys[2], (N_SECTION, TOKENS, D), 1.0, 6.0, ((0, 16), (1, 32)))
    norm_gain = jnp.clip(1.0 + 0.18 * jax.random.normal(arg_keys[3], (N_SECTION, D), jnp.float32), 0.1, 1.9)
    w_gate = bell_draw(arg_keys[4], (N_SECTION, D, EXPERTS * EXP_FF), D ** -0.5, 0.09375, ((0, 16), (2, 32)))
    w_up = bell_draw(arg_keys[5], (N_SECTION, D, EXPERTS * EXP_FF), D ** -0.5, 0.09375, ((0, 16), (2, 32)))
    w_down = bell_draw(arg_keys[6], (N_SECTION, EXPERTS * EXP_FF, D), EXP_FF ** -0.5, 0.1875, ((0, 16), (1, 32)))
    route_fwd_keys = jax.random.split(jax.random.fold_in(arg_keys[7], 1), N_SECTION * TOKENS // TOK)
    route_fwd_turns = jax.random.permutation(jax.random.fold_in(arg_keys[7], 3), N_SECTION * TOKENS // TOK)
    route_fwd = jax.vmap(lambda own, number: assign_block(jax.random.fold_in(arg_keys[7], 2), own, number, TOK, EXPERTS, 1, CAP, 2))(route_fwd_keys, route_fwd_turns).reshape((N_SECTION, TOKENS, 1))
    gate_fwd = plant(jax.random.randint(arg_keys[8], (N_SECTION, TOKENS, 1), 16, 256), jax.random.fold_in(arg_keys[8], 1), 16, 255).astype(jnp.int32)
    route_bwd_keys = jax.random.split(jax.random.fold_in(arg_keys[9], 1), N_SECTION * TOKENS // TOK)
    route_bwd_turns = jax.random.permutation(jax.random.fold_in(arg_keys[9], 3), N_SECTION * TOKENS // TOK)
    route_bwd = jax.vmap(lambda own, number: assign_block(jax.random.fold_in(arg_keys[9], 2), own, number, TOK, EXPERTS, 1, CAP, 2))(route_bwd_keys, route_bwd_turns).reshape((N_SECTION, TOKENS, 1))
    gate_bwd = plant(jax.random.randint(arg_keys[10], (N_SECTION, TOKENS, 1), 16, 256), jax.random.fold_in(arg_keys[10], 1), 16, 255).astype(jnp.int32)
    return {"x_fwd": x_fwd, "x_bwd": x_bwd, "grad_out": grad_out, "norm_gain": norm_gain, "w_gate": w_gate, "w_up": w_up, "w_down": w_down, "route_fwd": route_fwd, "gate_fwd": gate_fwd, "route_bwd": route_bwd, "gate_bwd": gate_bwd}


EPSILON = 1e-06

def rms_scale(values):
    return lax.rsqrt(lax.optimization_barrier(jnp.mean(values * values, axis=-1, keepdims=True)) + EPSILON)

def normalize(tokens, gain):
    values = tokens.astype(jnp.float32)
    return (values * rms_scale(values) * gain.astype(jnp.float32)).astype(jnp.bfloat16)

def norm_backward(tokens, gain, upstream):
    values = tokens.astype(jnp.float32)
    scale = rms_scale(values)
    weighted = upstream * gain.astype(jnp.float32)
    inner = lax.optimization_barrier(jnp.mean(values * weighted, axis=-1, keepdims=True))
    return scale * weighted - values * scale * scale * scale * inner

def slot_parts(route):
    table = route.reshape(N_EXPERT, TOK).astype(jnp.int32)
    onehot = (table[:, :, None] == jnp.arange(EXPERTS, dtype=jnp.int32)[None, None, :]).astype(jnp.int32)
    rank = lax.optimization_barrier(jnp.sum(jnp.cumsum(onehot, axis=1) * onehot, axis=2)) - 1
    device = jnp.broadcast_to(jnp.arange(N_EXPERT, dtype=jnp.int32)[:, None], (N_EXPERT, TOK))
    return (table, device, rank.astype(jnp.int32))

def place_rows(rows, table, device, rank):
    buffer = jnp.zeros((EXPERTS, N_EXPERT, CAP, D), jnp.bfloat16)
    return buffer.at[table, device, rank].set(rows.reshape(N_EXPERT, TOK, D))

def pick_rows(result, table, device, rank):
    return result[table, device, rank].reshape(N_EXPERT * TOK, D)

def round_sum(parts):
    rounded = lax.optimization_barrier(parts.astype(jnp.bfloat16))
    return lax.optimization_barrier(jnp.sum(rounded.astype(jnp.float32), axis=2))

def expert_forward(rows, gate_cols, up_cols, down_rows):
    rows32 = rows.astype(jnp.float32)
    gate = jnp.einsum('ncd,df->ncf', rows32, gate_cols.astype(jnp.float32))
    up = jnp.einsum('ncd,df->ncf', rows32, up_cols.astype(jnp.float32))
    act = (jax.nn.silu(gate) * up).astype(jnp.bfloat16)
    blocks = act.astype(jnp.float32).reshape(N_EXPERT, CAP, SPLIT, HID_DEV)
    down = down_rows.astype(jnp.float32).reshape(SPLIT, HID_DEV, D)
    return round_sum(jnp.einsum('ncsh,shd->ncsd', blocks, down))

def expert_backward(rows, grads, gate_cols, up_cols, down_rows):
    rows32 = rows.astype(jnp.float32)
    gate = jnp.einsum('ncd,df->ncf', rows32, gate_cols.astype(jnp.float32))
    up = jnp.einsum('ncd,df->ncf', rows32, up_cols.astype(jnp.float32))
    d_act = jnp.einsum('ncd,fd->ncf', grads.astype(jnp.float32), down_rows.astype(jnp.float32))
    sig = jax.nn.sigmoid(gate)
    d_gate = (d_act * up * sig * (1.0 + gate * (1.0 - sig))).astype(jnp.bfloat16)
    d_up = (d_act * gate * sig).astype(jnp.bfloat16)
    gate_blocks = d_gate.astype(jnp.float32).reshape(N_EXPERT, CAP, SPLIT, HID_DEV)
    up_blocks = d_up.astype(jnp.float32).reshape(N_EXPERT, CAP, SPLIT, HID_DEV)
    gate_w = gate_cols.astype(jnp.float32).reshape(D, SPLIT, HID_DEV)
    up_w = up_cols.astype(jnp.float32).reshape(D, SPLIT, HID_DEV)
    parts = jnp.einsum('ncsh,dsh->ncsd', gate_blocks, gate_w) + jnp.einsum('ncsh,dsh->ncsd', up_blocks, up_w)
    return round_sum(parts)

def section_work(items):
    x_fwd, x_bwd, grad_out, gain, w_gate, w_up, w_down, route_fwd, gate_fwd, route_bwd, gate_bwd = items
    gate_all = w_gate.reshape(D, EXPERTS, EXP_FF).transpose(1, 0, 2)
    up_all = w_up.reshape(D, EXPERTS, EXP_FF).transpose(1, 0, 2)
    down_all = w_down.reshape(EXPERTS, EXP_FF, D)
    normed_fwd = normalize(x_fwd, gain)
    table_f, device_f, rank_f = slot_parts(route_fwd[:, 0])
    buffer_f = place_rows(normed_fwd, table_f, device_f, rank_f)
    result_f = lax.map(lambda item: expert_forward(*item), (buffer_f, gate_all, up_all, down_all))
    moe_fwd = pick_rows(result_f, table_f, device_f, rank_f)
    scale_f = gate_fwd.astype(jnp.float32) / 256.0
    y_section = (x_fwd.astype(jnp.float32) + scale_f * moe_fwd).astype(jnp.bfloat16)
    normed_bwd = normalize(x_bwd, gain)
    scale_b = gate_bwd.astype(jnp.float32) / 256.0
    grad_rows = (grad_out.astype(jnp.float32) * scale_b).astype(jnp.bfloat16)
    table_b, device_b, rank_b = slot_parts(route_bwd[:, 0])
    buffer_b = place_rows(normed_bwd, table_b, device_b, rank_b)
    buffer_g = place_rows(grad_rows, table_b, device_b, rank_b)
    result_b = lax.map(lambda item: expert_backward(*item), (buffer_b, buffer_g, gate_all, up_all, down_all))
    d_normed = pick_rows(result_b, table_b, device_b, rank_b)
    dx_section = (grad_out.astype(jnp.float32) + norm_backward(x_bwd, gain, d_normed)).astype(jnp.bfloat16)
    return (y_section, dx_section)

def reference(x_fwd, x_bwd, grad_out, norm_gain, w_gate, w_up, w_down, route_fwd, gate_fwd, route_bwd, gate_bwd):
    y_section, dx_section = lax.map(section_work, (x_fwd, x_bwd, grad_out, norm_gain, w_gate, w_up, w_down, route_fwd, gate_fwd, route_bwd, gate_bwd))
    y_next = jnp.roll(y_section, 1, axis=0)
    dx_prev = jnp.roll(dx_section, -1, axis=0)
    return (y_next, dx_prev)
```

```python
import jax
import jax.numpy as jnp
from jax import lax
from jax.sharding import PartitionSpec as P

EXPERTS = 4
CAP = 12
EPSILON = 1e-06


def passed_along(value, axis, steps):
    count = lax.axis_size(axis)
    pairs = [(source, (source + steps) % count) for source in range(count)]
    return lax.ppermute(value, axis, pairs)


def rms_scale(values):
    return lax.rsqrt(jnp.mean(values * values, axis=-1, keepdims=True) + EPSILON)


def dot(a, b, dims):
    return lax.dot_general(a, b, (dims, ((), ())), preferred_element_type=jnp.float32)


def slots_of(route):
    onehot = (route[:, None] == jnp.arange(EXPERTS, dtype=jnp.int32)[None, :]).astype(jnp.int32)
    rank = jnp.sum(jnp.cumsum(onehot, axis=0) * onehot, axis=1) - 1
    return route * CAP + rank


def half_places(slot):
    expert, rank = slot // CAP, slot % CAP
    base = expert * (2 * CAP) + rank
    return [base + h * CAP for h in range(2)]


def pick_back(table, slot):
    rows = table.reshape(-1, table.shape[-1])
    count = rows.shape[0]
    halves = []
    for place in half_places(slot):
        pick = (place[:, None] == jnp.arange(count, dtype=jnp.int32)[None, :]).astype(jnp.bfloat16)
        halves.append(dot(pick, rows, ((1,), (0,))))
    return jnp.concatenate(halves, axis=1)


def packers(slots, me_expert, side):
    sources, tokens = slots.shape
    groups = sources // side
    expert, rank = slots // CAP, slots % CAP
    source = jnp.arange(sources, dtype=jnp.int32)[:, None]
    base = (source % side) * (groups * 2 * CAP) + (source // side) * (2 * CAP) + rank
    base = jnp.where(expert == me_expert, base, -2 * CAP)
    flat = base.reshape(-1)
    row = jnp.arange(sources * 2 * CAP, dtype=jnp.int32)[:, None]
    return [(flat[None, :] + h * CAP == row).astype(jnp.bfloat16) for h in range(2)]


def pack(places, hidden):
    parts = [dot(place, hidden, ((1,), (0,))).astype(jnp.bfloat16) for place in places]
    return jnp.concatenate(parts, axis=1)


def send_back(partial, side, within, across):
    rows, width = partial.shape
    blocks = partial.astype(jnp.bfloat16).reshape(side, rows // side, width)
    got = lax.all_to_all(
        blocks, "expert", split_axis=0, concat_axis=0, tiled=True, axis_index_groups=within
    )
    total = jnp.sum(got.astype(jnp.float32), axis=0).astype(jnp.bfloat16)
    total = total.reshape(EXPERTS, 2 * CAP, width)
    return lax.all_to_all(
        total, "expert", split_axis=0, concat_axis=0, tiled=True, axis_index_groups=across
    )


def per_device(
    x_fwd,
    x_bwd,
    grad_out,
    norm_gain,
    w_gate,
    w_up,
    w_down,
    route_fwd,
    gate_fwd,
    route_bwd,
    gate_bwd,
):
    count = lax.axis_size("expert")
    ring = count // 2
    side = ring // EXPERTS
    same_core = [[2 * z + c for z in range(ring)] for c in range(2)]
    within = [[2 * (side * g + j) + c for j in range(side)] for g in range(EXPERTS) for c in range(2)]
    across = [[2 * (side * g + j) + c for g in range(EXPERTS)] for j in range(side) for c in range(2)]
    swap = [(i, i ^ 1) for i in range(count)]
    me = lax.axis_index("expert") // (2 * side)

    gain = norm_gain[0]
    tokens, width = x_fwd.shape[1:]
    half = width // 2
    xf = x_fwd[0].astype(jnp.float32)
    xb = x_bwd[0].astype(jnp.float32)
    up32 = grad_out[0].astype(jnp.float32)
    scale_f = gate_fwd[0].astype(jnp.float32) / 256.0
    scale_b = gate_bwd[0].astype(jnp.float32) / 256.0
    r_b = rms_scale(xb)
    normed_f = (xf * rms_scale(xf) * gain).astype(jnp.bfloat16)
    normed_b = (xb * r_b * gain).astype(jnp.bfloat16)
    grad_rows = (up32 * scale_b).astype(jnp.bfloat16)
    slot_f = slots_of(route_fwd[0, :, 0])
    slot_b = slots_of(route_bwd[0, :, 0])

    sent = jnp.concatenate([normed_f, normed_b, grad_rows], axis=0)
    got = lax.all_gather(sent, "expert", axis=0, tiled=False, axis_index_groups=same_core)
    rows_f = got[:, :tokens].reshape(ring * tokens, width)
    rows_b = got[:, tokens : 2 * tokens].reshape(ring * tokens, width)
    rows_g = got[:, 2 * tokens :].reshape(ring * tokens, width)
    both = jnp.concatenate([slot_f, slot_b])
    slots = lax.all_to_all(
        jnp.broadcast_to(both[None, None, :], (ring, 1, 2 * tokens)),
        "expert",
        split_axis=0,
        concat_axis=0,
        tiled=True,
        axis_index_groups=same_core,
    )[:, 0]

    gate_o = lax.ppermute(w_gate[0], "expert", swap)
    up_o = lax.ppermute(w_up[0], "expert", swap)
    down_o = lax.ppermute(w_down[0], "expert", swap)
    w_in = jnp.concatenate([w_gate[0], gate_o, w_up[0], up_o], axis=1)
    w_dn = jnp.concatenate([w_down[0], down_o], axis=0)
    hid = w_dn.shape[0]
    dn_stack = jnp.concatenate([w_dn[:, :half], w_dn[:, half:]], axis=0)
    in_stack = jnp.concatenate([w_in[:half], w_in[half:]], axis=1)

    place_f = packers(slots[:, :tokens], me, side)
    place_b = packers(slots[:, tokens:], me, side)

    pre_f = dot(rows_f, w_in, ((1,), (0,)))
    act = (jax.nn.silu(pre_f[:, :hid]) * pre_f[:, hid:]).astype(jnp.bfloat16)
    part_f = dot(pack(place_f, act), dn_stack, ((1,), (0,)))
    table_f = send_back(part_f, side, within, across)

    pre_b = dot(rows_b, w_in, ((1,), (0,)))
    d_act = dot(rows_g, w_dn, ((1,), (1,)))
    gate, up = pre_b[:, :hid], pre_b[:, hid:]
    sig = jax.nn.sigmoid(gate)
    d_gate = (d_act * up * sig * (1.0 + gate * (1.0 - sig))).astype(jnp.bfloat16)
    d_up = (d_act * gate * sig).astype(jnp.bfloat16)
    part_b = dot(pack(place_b, jnp.concatenate([d_gate, d_up], axis=1)), in_stack, ((1,), (1,)))
    table_b = send_back(part_b, side, within, across)

    moe_f = pick_back(table_f, slot_f)
    y = (xf + scale_f * moe_f).astype(jnp.bfloat16)
    d_normed = pick_back(table_b, slot_b)
    weighted = d_normed * gain
    inner = jnp.mean(xb * weighted, axis=-1, keepdims=True)
    dx = (up32 + (r_b * weighted - xb * r_b * r_b * r_b * inner)).astype(jnp.bfloat16)
    y_next = passed_along(y, "section", 1)
    dx_prev = passed_along(dx, "section", -1)
    return (y_next[None], dx_prev[None])


def solution(mesh):
    in_specs = (
        P("section", "expert", None),
        P("section", "expert", None),
        P("section", "expert", None),
        P("section", None),
        P("section", None, "expert"),
        P("section", None, "expert"),
        P("section", "expert", None),
        P("section", "expert", None),
        P("section", "expert", None),
        P("section", "expert", None),
        P("section", "expert", None),
    )
    out_specs = (P("section", "expert", None), P("section", "expert", None))
    return jax.shard_map(
        per_device, mesh=mesh, in_specs=in_specs, out_specs=out_specs, check_vma=False
    )
```

```python
import jax
import jax.numpy as jnp
from jax import lax
from jax.sharding import PartitionSpec as P

EXPERTS = 4
CAP = 12
EPSILON = 1e-06


def passed_along(value, axis, steps):
    count = lax.axis_size(axis)
    pairs = [(source, (source + steps) % count) for source in range(count)]
    return lax.ppermute(value, axis, pairs)


def rms_scale(values):
    return lax.rsqrt(jnp.mean(values * values, axis=-1, keepdims=True) + EPSILON)


def dot(a, b, dims):
    return lax.dot_general(a, b, (dims, ((), ())), preferred_element_type=jnp.float32)


def slots_of(route):
    onehot = (route[:, None] == jnp.arange(EXPERTS, dtype=jnp.int32)[None, :]).astype(jnp.int32)
    rank = jnp.sum(jnp.cumsum(onehot, axis=0) * onehot, axis=1) - 1
    return route * CAP + rank


def half_places(slot):
    expert, rank = slot // CAP, slot % CAP
    base = expert * (2 * CAP) + rank
    return [base + h * CAP for h in range(2)]


def pick_back(table, slot):
    rows = table.reshape(-1, table.shape[-1])
    count = rows.shape[0]
    halves = []
    for place in half_places(slot):
        pick = (place[:, None] == jnp.arange(count, dtype=jnp.int32)[None, :]).astype(jnp.bfloat16)
        halves.append(dot(pick, rows, ((1,), (0,))))
    return jnp.concatenate(halves, axis=1)


def shifts(count, side, steps):
    pairs = []
    for device in range(count):
        chip, core = device // 2, device % 2
        place = chip // side * side + (chip % side + steps) % side
        pairs.append((device, 2 * place + core))
    return pairs


def packers(slots, me_expert, me_place, tokens, side):
    count = slots.shape[0]
    sources = count // tokens
    groups = sources // side
    expert, rank = slots // CAP, slots % CAP
    source = jnp.arange(count, dtype=jnp.int32) // tokens
    back = (me_place - source % side) % side
    base = back * (groups * 2 * CAP) + (source // side) * (2 * CAP) + rank
    base = jnp.where(expert == me_expert, base, -2 * CAP)
    row = jnp.arange(sources * 2 * CAP, dtype=jnp.int32)[:, None]
    return [(base[None, :] + h * CAP == row).astype(jnp.bfloat16) for h in range(2)]


def join_group(partial, count, side):
    rows, width = partial.shape
    part = rows // side
    blocks = partial.astype(jnp.bfloat16)
    total = blocks[:part].astype(jnp.float32)
    for k in range(1, side):
        got = lax.ppermute(blocks[k * part : (k + 1) * part], "expert", shifts(count, side, -k))
        total = total + got.astype(jnp.float32)
    return total.astype(jnp.bfloat16).reshape(EXPERTS, 2 * CAP, width)


def across_groups(blocks, across):
    return lax.all_to_all(
        blocks, "expert", split_axis=0, concat_axis=0, tiled=True, axis_index_groups=across
    )


def per_device(
    x_fwd,
    x_bwd,
    grad_out,
    norm_gain,
    w_gate,
    w_up,
    w_down,
    route_fwd,
    gate_fwd,
    route_bwd,
    gate_bwd,
):
    count = lax.axis_size("expert")
    ring = count // 2
    side = ring // EXPERTS
    same_core = [[2 * z + c for z in range(ring)] for c in range(2)]
    across = [[2 * (side * g + j) + c for g in range(EXPERTS)] for j in range(side) for c in range(2)]
    swap = [(i, i ^ 1) for i in range(count)]
    index = lax.axis_index("expert")
    me_expert = index // (2 * side)
    me_place = (index // 2) % side

    gain = norm_gain[0]
    tokens, width = x_fwd.shape[1:]
    half = width // 2
    xf = x_fwd[0].astype(jnp.float32)
    xb = x_bwd[0].astype(jnp.float32)
    up32 = grad_out[0].astype(jnp.float32)
    scale_f = gate_fwd[0].astype(jnp.float32) / 256.0
    scale_b = gate_bwd[0].astype(jnp.float32) / 256.0
    r_b = rms_scale(xb)
    slot_f = slots_of(route_fwd[0, :, 0])
    slot_b = slots_of(route_bwd[0, :, 0])

    normed_b = (xb * r_b * gain).astype(jnp.bfloat16)
    grad_rows = (up32 * scale_b).astype(jnp.bfloat16)
    tag = jnp.broadcast_to(slot_b[:, None].astype(jnp.bfloat16), (tokens, 128))
    sent = jnp.concatenate([normed_b, grad_rows, tag], axis=1)
    got = lax.all_gather(sent, "expert", axis=0, tiled=True, axis_index_groups=same_core)

    normed_f = (xf * rms_scale(xf) * gain).astype(jnp.bfloat16)
    place = jnp.concatenate(half_places(slot_f))
    table_row = jnp.arange(EXPERTS * 2 * CAP, dtype=jnp.int32)[:, None]
    put = (place[None, :] == table_row).astype(jnp.bfloat16)
    halves = jnp.concatenate([normed_f[:, :half], normed_f[:, half:]], axis=0)
    packed = dot(put, halves, ((1,), (0,))).astype(jnp.bfloat16)
    mine = across_groups(packed.reshape(EXPERTS, 2 * CAP, half), across)
    mine = mine.reshape(EXPERTS * 2 * CAP, half)
    blocks = [mine] + [lax.ppermute(mine, "expert", shifts(count, side, k)) for k in range(1, side)]
    rows_f = jnp.concatenate(blocks, axis=0)

    gate_o = lax.ppermute(w_gate[0], "expert", swap)
    up_o = lax.ppermute(w_up[0], "expert", swap)
    down_o = lax.ppermute(w_down[0], "expert", swap)
    w_in = jnp.concatenate([w_gate[0], gate_o, w_up[0], up_o], axis=1)
    w_dn = jnp.concatenate([w_down[0], down_o], axis=0)
    hid = w_dn.shape[0]
    dn_stack = jnp.concatenate([w_dn[:, :half], w_dn[:, half:]], axis=0)
    in_stack = jnp.concatenate([w_in[:half], w_in[half:]], axis=1)

    pre_f = dot(rows_f, in_stack, ((1,), (0,))).reshape(ring, 2 * CAP, 4 * hid)
    pre_f = pre_f[:, :CAP, : 2 * hid] + pre_f[:, CAP:, 2 * hid :]
    act = (jax.nn.silu(pre_f[..., :hid]) * pre_f[..., hid:]).astype(jnp.bfloat16)
    lower = jnp.pad(act, ((0, 0), (0, CAP), (0, 0)))
    upper = jnp.pad(act, ((0, 0), (CAP, 0), (0, 0)))
    act = jnp.concatenate([lower, upper], axis=2).reshape(ring * 2 * CAP, 2 * hid)
    part_f = dot(act, dn_stack, ((1,), (0,)))
    total_f = join_group(part_f, count, side)
    got, total_f = lax.optimization_barrier((got, total_f))
    table_f = across_groups(total_f, across)

    rows_b = got[:, :width]
    rows_g = got[:, width : 2 * width]
    slots_b = got[:, 2 * width].astype(jnp.int32)
    pre_b = dot(rows_b, w_in, ((1,), (0,)))
    d_act = dot(rows_g, w_dn, ((1,), (1,)))
    gate, up = pre_b[:, :hid], pre_b[:, hid:]
    sig = jax.nn.sigmoid(gate)
    d_gate = (d_act * up * sig * (1.0 + gate * (1.0 - sig))).astype(jnp.bfloat16)
    d_up = (d_act * gate * sig).astype(jnp.bfloat16)
    hidden_b = jnp.concatenate([d_gate, d_up], axis=1)
    places = packers(slots_b, me_expert, me_place, tokens, side)
    parts = [dot(p, hidden_b, ((1,), (0,))).astype(jnp.bfloat16) for p in places]
    part_b = dot(jnp.concatenate(parts, axis=1), in_stack, ((1,), (1,)))
    table_b = across_groups(join_group(part_b, count, side), across)

    moe_f = pick_back(table_f, slot_f)
    y = (xf + scale_f * moe_f).astype(jnp.bfloat16)
    d_normed = pick_back(table_b, slot_b)
    weighted = d_normed * gain
    inner = jnp.mean(xb * weighted, axis=-1, keepdims=True)
    dx = (up32 + (r_b * weighted - xb * r_b * r_b * r_b * inner)).astype(jnp.bfloat16)
    y_next = passed_along(y, "section", 1)
    dx_prev = passed_along(dx, "section", -1)
    return (y_next[None], dx_prev[None])


def solution(mesh):
    in_specs = (
        P("section", "expert", None),
        P("section", "expert", None),
        P("section", "expert", None),
        P("section", None),
        P("section", None, "expert"),
        P("section", None, "expert"),
        P("section", "expert", None),
        P("section", "expert", None),
        P("section", "expert", None),
        P("section", "expert", None),
        P("section", "expert", None),
    )
    out_specs = (P("section", "expert", None), P("section", "expert", None))
    return jax.shard_map(
        per_device, mesh=mesh, in_specs=in_specs, out_specs=out_specs, check_vma=False
    )
```

```python
import jax
import jax.numpy as jnp
from jax import lax
from jax.sharding import PartitionSpec as P

EXPERTS = 4
CAP = 12
EPSILON = 1e-06


def passed_along(value, axis, steps):
    count = lax.axis_size(axis)
    pairs = [(source, (source + steps) % count) for source in range(count)]
    return lax.ppermute(value, axis, pairs)


def rms_scale(values):
    return lax.rsqrt(jnp.mean(values * values, axis=-1, keepdims=True) + EPSILON)


def dot(a, b, dims):
    return lax.dot_general(a, b, (dims, ((), ())), preferred_element_type=jnp.float32)


def slots_of(route):
    onehot = (route[:, None] == jnp.arange(EXPERTS, dtype=jnp.int32)[None, :]).astype(jnp.int32)
    rank = jnp.sum(jnp.cumsum(onehot, axis=0) * onehot, axis=1) - 1
    return route * CAP + rank


def half_places(slot):
    expert, rank = slot // CAP, slot % CAP
    base = expert * (2 * CAP) + rank
    return [base + h * CAP for h in range(2)]


def pick_back(table, slot):
    rows = table.reshape(-1, table.shape[-1])
    count = rows.shape[0]
    halves = []
    for place in half_places(slot):
        pick = (place[:, None] == jnp.arange(count, dtype=jnp.int32)[None, :]).astype(jnp.bfloat16)
        halves.append(dot(pick, rows, ((1,), (0,))))
    return jnp.concatenate(halves, axis=1)


def shifts(count, side, steps):
    pairs = []
    for device in range(count):
        chip, core = device // 2, device % 2
        place = chip // side * side + (chip % side + steps) % side
        pairs.append((device, 2 * place + core))
    return pairs


def shifts(count, side, steps):
    pairs = []
    for device in range(count):
        chip, core = device // 2, device % 2
        place = chip // side * side + (chip % side + steps) % side
        pairs.append((device, 2 * place + core))
    return pairs


def packers(slots, me_expert, me_place, tokens, side):
    count = slots.shape[0]
    sources = count // tokens
    groups = sources // side
    expert, rank = slots // CAP, slots % CAP
    source = jnp.arange(count, dtype=jnp.int32) // tokens
    back = (me_place - source % side) % side
    base = back * (groups * 2 * CAP) + (source // side) * (2 * CAP) + rank
    base = jnp.where(expert == me_expert, base, -2 * CAP)
    row = jnp.arange(sources * 2 * CAP, dtype=jnp.int32)[:, None]
    return [(base[None, :] + h * CAP == row).astype(jnp.bfloat16) for h in range(2)]


def join_group(partial, count, side):
    rows, width = partial.shape
    part = rows // side
    blocks = partial.astype(jnp.bfloat16)
    total = blocks[:part].astype(jnp.float32)
    for k in range(1, side):
        got = lax.ppermute(blocks[k * part : (k + 1) * part], "expert", shifts(count, side, -k))
        total = total + got.astype(jnp.float32)
    return total.astype(jnp.bfloat16).reshape(EXPERTS, 2 * CAP, width)


def across_groups(blocks, across):
    return lax.all_to_all(
        blocks, "expert", split_axis=0, concat_axis=0, tiled=True, axis_index_groups=across
    )


def per_device(
    x_fwd,
    x_bwd,
    grad_out,
    norm_gain,
    w_gate,
    w_up,
    w_down,
    route_fwd,
    gate_fwd,
    route_bwd,
    gate_bwd,
):
    count = lax.axis_size("expert")
    ring = count // 2
    side = ring // EXPERTS
    same_core = [[2 * z + c for z in range(ring)] for c in range(2)]
    across = [[2 * (side * g + j) + c for g in range(EXPERTS)] for j in range(side) for c in range(2)]
    swap = [(i, i ^ 1) for i in range(count)]
    index = lax.axis_index("expert")
    me_expert = index // (2 * side)
    me_place = (index // 2) % side

    gain = norm_gain[0]
    tokens, width = x_fwd.shape[1:]
    half = width // 2
    sent = jnp.concatenate([x_fwd[0], x_bwd[0], grad_out[0]], axis=1)
    got = lax.all_gather(sent, "expert", axis=0, tiled=True, axis_index_groups=same_core)

    xf = x_fwd[0].astype(jnp.float32)
    xb = x_bwd[0].astype(jnp.float32)
    up32 = grad_out[0].astype(jnp.float32)
    scale_f = gate_fwd[0].astype(jnp.float32) / 256.0
    scale_b = gate_bwd[0].astype(jnp.float32) / 256.0
    r_f = rms_scale(xf)
    r_b = rms_scale(xb)
    slot_f = slots_of(route_fwd[0, :, 0])
    slot_b = slots_of(route_bwd[0, :, 0])
    small = jnp.concatenate(
        [slot_f.astype(jnp.float32), slot_b.astype(jnp.float32), r_f[:, 0], r_b[:, 0], scale_b[:, 0]]
    )
    small = lax.all_to_all(
        jnp.broadcast_to(small[None, None, :], (ring, 1, 5 * tokens)),
        "expert",
        split_axis=0,
        concat_axis=0,
        tiled=True,
        axis_index_groups=same_core,
    )[:, 0]
    slots_f, slots_b, rs_f, rs_b, scales_b = [
        small[:, i * tokens : (i + 1) * tokens].reshape(ring * tokens) for i in range(5)
    ]
    slots_f = slots_f.astype(jnp.int32)
    slots_b = slots_b.astype(jnp.int32)

    gate_o = lax.ppermute(w_gate[0], "expert", swap)
    up_o = lax.ppermute(w_up[0], "expert", swap)
    down_o = lax.ppermute(w_down[0], "expert", swap)
    w_in = jnp.concatenate([w_gate[0], gate_o, w_up[0], up_o], axis=1)
    w_gained = (w_in.astype(jnp.float32) * gain[:, None]).astype(jnp.bfloat16)
    w_dn = jnp.concatenate([w_down[0], down_o], axis=0)
    hid = w_dn.shape[0]
    in_stack = jnp.concatenate([w_in[:half], w_in[half:]], axis=1)
    w_gained, w_dn, in_stack = lax.optimization_barrier((w_gained, w_dn, in_stack))

    pre_f = dot(got[:, :width], w_gained, ((1,), (0,))) * rs_f[:, None]
    act = jax.nn.silu(pre_f[:, :hid]) * pre_f[:, hid:]
    act = jnp.where((slots_f // CAP == me_expert)[:, None], act, 0.0).astype(jnp.bfloat16)
    part_f = dot(act, w_dn, ((1,), (0,))).astype(jnp.bfloat16)
    got, part_f = lax.optimization_barrier((got, part_f))
    moe_f = lax.psum_scatter(
        part_f, "expert", scatter_dimension=0, tiled=True, axis_index_groups=same_core
    )

    pre_b = dot(got[:, width : 2 * width], w_gained, ((1,), (0,))) * rs_b[:, None]
    d_act = dot(got[:, 2 * width :], w_dn, ((1,), (1,))) * scales_b[:, None]
    gate, up = pre_b[:, :hid], pre_b[:, hid:]
    sig = jax.nn.sigmoid(gate)
    d_gate = (d_act * up * sig * (1.0 + gate * (1.0 - sig))).astype(jnp.bfloat16)
    d_up = (d_act * gate * sig).astype(jnp.bfloat16)
    hidden_b = jnp.concatenate([d_gate, d_up], axis=1)
    places = packers(slots_b, me_expert, me_place, tokens, side)
    parts = [dot(p, hidden_b, ((1,), (0,))).astype(jnp.bfloat16) for p in places]
    part_b = dot(jnp.concatenate(parts, axis=1), in_stack, ((1,), (1,)))
    table_b = across_groups(join_group(part_b, count, side), across)

    y = (xf + scale_f * moe_f.astype(jnp.float32)).astype(jnp.bfloat16)
    d_normed = pick_back(table_b, slot_b)
    weighted = d_normed * gain
    inner = jnp.mean(xb * weighted, axis=-1, keepdims=True)
    dx = (up32 + (r_b * weighted - xb * r_b * r_b * r_b * inner)).astype(jnp.bfloat16)
    y_next = passed_along(y, "section", 1)
    dx_prev = passed_along(dx, "section", -1)
    return (y_next[None], dx_prev[None])


def solution(mesh):
    in_specs = (
        P("section", "expert", None),
        P("section", "expert", None),
        P("section", "expert", None),
        P("section", None),
        P("section", None, "expert"),
        P("section", None, "expert"),
        P("section", "expert", None),
        P("section", "expert", None),
        P("section", "expert", None),
        P("section", "expert", None),
        P("section", "expert", None),
    )
    out_specs = (P("section", "expert", None), P("section", "expert", None))
    return jax.shard_map(
        per_device, mesh=mesh, in_specs=in_specs, out_specs=out_specs, check_vma=False
    )
```

```python
import jax
import jax.numpy as jnp
import numpy as np
from jax import lax
from jax.sharding import PartitionSpec as P

EXPERTS = 4
CAP = 12
EPSILON = 1e-06


def passed_along(value, axis, steps):
    count = lax.axis_size(axis)
    pairs = [(source, (source + steps) % count) for source in range(count)]
    return lax.ppermute(value, axis, pairs)


def rms_scale(values):
    return lax.rsqrt(jnp.mean(values * values, axis=-1, keepdims=True) + EPSILON)


def dot(a, b, dims):
    return lax.dot_general(a, b, (dims, ((), ())), preferred_element_type=jnp.float32)


def slots_of(route):
    onehot = (route[:, None] == jnp.arange(EXPERTS, dtype=jnp.int32)[None, :]).astype(jnp.int32)
    rank = jnp.sum(jnp.cumsum(onehot, axis=0) * onehot, axis=1) - 1
    return route * CAP + rank


PREFIX = (3, 2, 2, 2, 2, 1, 1, 1, 1)
UNIT = 2 * CAP
SIDE = 4


def right_list(place):
    return [1, 0, -1] if place < SIDE // 2 else [2, 1, 0]


def left_list(place):
    return [3, 0, -1] if place >= SIDE // 2 else [2, 3, 0]


def list_tables():
    sent, valid = [], []
    for place in range(SIDE):
        sent.append(right_list(place) + left_list(place) + [0])
        flags = []
        for step, size in enumerate(PREFIX, 1):
            crossed = max(0, -((place - step) // SIDE))
            units = right_list((place - step) % SIDE)[:size]
            flags += [int(unit == crossed) for unit in units]
        for step, size in enumerate(PREFIX, 1):
            crossed = max(0, (place + step) // SIDE)
            units = left_list((place + step) % SIDE)[:size]
            flags += [int(unit == (EXPERTS - crossed) % EXPERTS) for unit in units]
        both, at = [], 0
        for size in PREFIX:
            both += flags[at : at + size] + flags[at + sum(PREFIX) : at + sum(PREFIX) + size]
            at += size
        valid.append(both + [1])
    return np.array(sent, np.int32), np.array(valid, np.float32)


def along_ring(count, steps):
    chips = count // 2
    return [(d, 2 * ((d // 2 + steps) % chips) + d % 2) for d in range(count)]


def walk_out(units, pairs):
    came = []
    for size in PREFIX:
        units = lax.ppermute(units[: size * UNIT], "expert", pairs)
        came.append(units)
    return came


def walk_back(parts, to_left, to_right):
    total = parts[-1]
    for step in range(len(PREFIX) - 1, -1, -1):
        rows = PREFIX[step] * UNIT
        back_r = lax.ppermute(total[:rows], "expert", to_left)
        back_l = lax.ppermute(total[rows:], "expert", to_right)
        if step > 0:
            extra = (PREFIX[step - 1] - PREFIX[step]) * UNIT
            pad = [jnp.pad(got, ((0, extra), (0, 0))) for got in (back_r, back_l)]
            total = parts[step - 1].astype(jnp.float32) + jnp.concatenate(pad).astype(jnp.float32)
            total = total.astype(jnp.bfloat16)
    return back_r, back_l


def per_device(
    x_fwd,
    x_bwd,
    grad_out,
    norm_gain,
    w_gate,
    w_up,
    w_down,
    route_fwd,
    gate_fwd,
    route_bwd,
    gate_bwd,
):
    count = lax.axis_size("expert")
    ring = count // 2
    same_core = [[2 * z + c for z in range(ring)] for c in range(2)]
    to_right, to_left = along_ring(count, 1), along_ring(count, -1)
    swap = [(i, i ^ 1) for i in range(count)]
    index = lax.axis_index("expert")
    me_expert = index // (2 * SIDE)
    me_place = (index // 2) % SIDE
    sent_table, valid_table = list_tables()
    groups_sent = jnp.asarray(sent_table)[me_place]
    valid = jnp.asarray(valid_table)[me_place]

    gain = norm_gain[0]
    tokens, width = x_fwd.shape[1:]
    half = width // 2
    sent = jnp.concatenate([x_bwd[0], grad_out[0]], axis=1)
    got_b = lax.all_gather(sent, "expert", axis=0, tiled=True, axis_index_groups=same_core)

    xf = x_fwd[0].astype(jnp.float32)
    xb = x_bwd[0].astype(jnp.float32)
    up32 = grad_out[0].astype(jnp.float32)
    scale_f = gate_fwd[0].astype(jnp.float32) / 256.0
    scale_b = gate_bwd[0].astype(jnp.float32) / 256.0

    normed_f = (xf * rms_scale(xf) * gain).astype(jnp.bfloat16)
    slot_f = slots_of(route_fwd[0, :, 0])
    unit_f = (slot_f // CAP - me_expert) % EXPERTS
    rank_f = slot_f % CAP
    row = jnp.arange(7 * UNIT, dtype=jnp.int32)
    row_unit = jnp.repeat(groups_sent, UNIT, total_repeat_length=7 * UNIT)
    row_slot = jnp.where(row_unit < 0, -1, row_unit * UNIT + row % UNIT)
    want = jnp.concatenate([unit_f * UNIT + rank_f, unit_f * UNIT + rank_f + CAP])
    put = (row_slot[:, None] == want[None, :]).astype(jnp.bfloat16)
    halves = jnp.concatenate([normed_f[:, :half], normed_f[:, half:]], axis=0)
    packed = dot(put, halves, ((1,), (0,))).astype(jnp.bfloat16)
    came_r = walk_out(packed[: 3 * UNIT], to_right)
    came_l = walk_out(packed[3 * UNIT : 6 * UNIT], to_left)
    came = [rows for pair in zip(came_r, came_l) for rows in pair]
    rows_f = jnp.concatenate(came + [packed[6 * UNIT :]], axis=0)

    r_b = rms_scale(xb)
    small = jnp.concatenate(
        [route_bwd[0, :, 0].astype(jnp.float32), r_b[:, 0], scale_b[:, 0]]
    )
    small, _ = lax.optimization_barrier((small, came_r[1]))
    small = lax.all_to_all(
        jnp.broadcast_to(small[None, None, :], (ring, 1, 3 * tokens)),
        "expert",
        split_axis=0,
        concat_axis=0,
        tiled=True,
        axis_index_groups=same_core,
    )[:, 0]
    routes_b, rs_b, scales_b = [
        small[:, i * tokens : (i + 1) * tokens].reshape(ring * tokens) for i in range(3)
    ]

    gate_o = lax.ppermute(w_gate[0], "expert", swap)
    up_o = lax.ppermute(w_up[0], "expert", swap)
    down_o = lax.ppermute(w_down[0], "expert", swap)
    w_in = jnp.concatenate([w_gate[0], gate_o, w_up[0], up_o], axis=1)
    w_gained = (w_in.astype(jnp.float32) * gain[:, None]).astype(jnp.bfloat16)
    w_dn = jnp.concatenate([w_down[0], down_o], axis=0)
    hid = w_dn.shape[0]
    dn_stack = jnp.concatenate([w_dn[:, :half], w_dn[:, half:]], axis=0)
    in_stack = jnp.concatenate([w_in[:half], w_in[half:]], axis=1)
    w_in, w_gained, w_dn, in_stack, dn_stack = lax.optimization_barrier(
        (w_in, w_gained, w_dn, in_stack, dn_stack)
    )

    units = valid.shape[0]
    pre_f = dot(rows_f, in_stack, ((1,), (0,))).reshape(units, UNIT, 4 * hid)
    pre_f = pre_f[:, :CAP, : 2 * hid] + pre_f[:, CAP:, 2 * hid :]
    act = jax.nn.silu(pre_f[..., :hid]) * pre_f[..., hid:]
    act = jnp.where(valid[:, None, None] > 0, act, 0.0).astype(jnp.bfloat16)
    lower = jnp.pad(act, ((0, 0), (0, CAP), (0, 0)))
    upper = jnp.pad(act, ((0, 0), (CAP, 0), (0, 0)))
    act = jnp.concatenate([lower, upper], axis=2).reshape(units * UNIT, 2 * hid)
    part_f = dot(act, dn_stack, ((1,), (0,))).astype(jnp.bfloat16)
    got_b, part_f = lax.optimization_barrier((got_b, part_f))

    pre_b = dot(got_b[:, :width], w_gained, ((1,), (0,))) * rs_b[:, None]
    d_act = dot(got_b[:, width:], w_dn, ((1,), (1,))) * scales_b[:, None]
    gate, up = pre_b[:, :hid], pre_b[:, hid:]
    sig = jax.nn.sigmoid(gate)
    mine = (routes_b == me_expert.astype(jnp.float32))[:, None]
    d_gate = jnp.where(mine, d_act * up * sig * (1.0 + gate * (1.0 - sig)), 0.0)
    d_up = jnp.where(mine, d_act * gate * sig, 0.0)
    hidden_b = jnp.concatenate([d_gate.astype(jnp.bfloat16), d_up.astype(jnp.bfloat16)], axis=1)
    part_b = dot(hidden_b, w_in, ((1,), (1,))).astype(jnp.bfloat16)
    d_normed = lax.psum_scatter(
        part_b, "expert", scatter_dimension=0, tiled=True, axis_index_groups=same_core
    ).astype(jnp.float32)

    seen = part_b[0, 0].astype(jnp.float32)
    never = (seen > 1.0) & (seen < -1.0)
    ends = np.cumsum([2 * size * UNIT for size in PREFIX]).tolist()
    starts = [0] + ends[:-1]
    pieces = [part_f[lo:hi] for lo, hi in zip(starts, ends)]
    pieces[-1] = jnp.where(never, 0, pieces[-1])
    back_r, back_l = walk_back(pieces, to_left, to_right)
    table = jnp.concatenate([back_r, back_l, part_f[ends[-1] :]], axis=0)
    moe_f = dot(put, table, ((0,), (0,)))
    moe_f = jnp.concatenate([moe_f[:tokens], moe_f[tokens:]], axis=1)
    y = (xf + scale_f * moe_f).astype(jnp.bfloat16)

    weighted = d_normed * gain
    inner = jnp.mean(xb * weighted, axis=-1, keepdims=True)
    dx = (up32 + (r_b * weighted - xb * r_b * r_b * r_b * inner)).astype(jnp.bfloat16)
    y_next = passed_along(y, "section", 1)
    dx_prev = passed_along(dx, "section", -1)
    return (y_next[None], dx_prev[None])


def solution(mesh):
    in_specs = (
        P("section", "expert", None),
        P("section", "expert", None),
        P("section", "expert", None),
        P("section", None),
        P("section", None, "expert"),
        P("section", None, "expert"),
        P("section", "expert", None),
        P("section", "expert", None),
        P("section", "expert", None),
        P("section", "expert", None),
        P("section", "expert", None),
    )
    out_specs = (P("section", "expert", None), P("section", "expert", None))
    return jax.shard_map(
        per_device, mesh=mesh, in_specs=in_specs, out_specs=out_specs, check_vma=False
    )
```

```python
import jax
import jax.numpy as jnp
from jax import lax
from jax.sharding import PartitionSpec as P

EXPERTS = 4
CAP = 12
EPSILON = 1e-06


def passed_along(value, axis, steps):
    count = lax.axis_size(axis)
    pairs = [(source, (source + steps) % count) for source in range(count)]
    return lax.ppermute(value, axis, pairs)


def rms_scale(values):
    return lax.rsqrt(jnp.mean(values * values, axis=-1, keepdims=True) + EPSILON)


def dot(a, b, dims):
    return lax.dot_general(a, b, (dims, ((), ())), preferred_element_type=jnp.float32)


def slots_of(route):
    onehot = (route[:, None] == jnp.arange(EXPERTS, dtype=jnp.int32)[None, :]).astype(jnp.int32)
    rank = jnp.sum(jnp.cumsum(onehot, axis=0) * onehot, axis=1) - 1
    return route * CAP + rank


def along(count, chip_of):
    return [(d, 2 * chip_of(d // 2) + d % 2) for d in range(count)]


def in_group(count, side, place_of):
    return along(count, lambda chip: chip // side * side + place_of(chip % side))


def to_section(value, sections, count, steps, hop, chips):
    pairs = []
    for s in range(sections):
        for d in range(count):
            chip = (d // 2 + hop) % chips
            pairs.append((s * count + d, (s + steps) % sections * count + 2 * chip + d % 2))
    return lax.ppermute(value, ("section", "expert"), pairs)


def pick_rows(route, me_group):
    slot = slots_of(route)
    place = (slot // CAP - me_group) % EXPERTS * (2 * CAP) + slot % CAP
    want = jnp.concatenate([place, place + CAP])
    row = jnp.arange(EXPERTS * 2 * CAP, dtype=jnp.int32)[:, None]
    return (row == want[None, :]).astype(jnp.bfloat16)


def packers(slots, me_group, me_place, tokens, side):
    count = slots.shape[0]
    sources = count // tokens
    groups = sources // side
    expert, rank = slots // CAP, slots % CAP
    source = jnp.arange(count, dtype=jnp.int32) // tokens
    back = (me_place - source % side) % side
    base = (back * groups + (me_group - source // side) % groups) * (2 * CAP) + rank
    base = jnp.where(expert == me_group, base, -2 * CAP)
    row = jnp.arange(sources * 2 * CAP, dtype=jnp.int32)[:, None]
    return [(base[None, :] + h * CAP == row).astype(jnp.bfloat16) for h in range(2)]


def add(a, b):
    return (a.astype(jnp.float32) + b.astype(jnp.float32)).astype(jnp.bfloat16)


def per_device(
    x_fwd,
    x_bwd,
    grad_out,
    norm_gain,
    w_gate,
    w_up,
    w_down,
    route_fwd,
    gate_fwd,
    route_bwd,
    gate_bwd,
):
    sections = lax.axis_size("section")
    count = lax.axis_size("expert")
    ring = count // 2
    side = ring // EXPERTS
    unit = 2 * CAP
    part = EXPERTS * unit
    same_core = [[2 * z + c for z in range(ring)] for c in range(2)]
    near = in_group(count, side, lambda j: j ^ 1)
    far = in_group(count, side, lambda j: j ^ 2)
    swap = [(i, i ^ 1) for i in range(count)]
    index = lax.axis_index("expert")
    me_group = index // (2 * side)
    me_place = (index // 2) % side

    gain = norm_gain[0]
    tokens, width = x_fwd.shape[1:]
    half = width // 2
    sent = jnp.concatenate([x_bwd[0], grad_out[0]], axis=1)
    got_b = lax.all_gather(sent, "expert", axis=0, tiled=True, axis_index_groups=same_core)

    xf = x_fwd[0].astype(jnp.float32)
    normed_f = (xf * rms_scale(xf) * gain).astype(jnp.bfloat16)
    put = pick_rows(route_fwd[0, :, 0], me_group)
    halves = jnp.concatenate([normed_f[:, :half], normed_f[:, half:]], axis=0)
    packed = dot(put, halves, ((1,), (0,))).astype(jnp.bfloat16)
    blocks = [packed[:unit]]
    for k in range(1, EXPERTS):
        hop = along(count, lambda chip: (chip + side * k) % ring)
        blocks.append(lax.ppermute(packed[k * unit : (k + 1) * unit], "expert", hop))
    mine = jnp.concatenate(blocks, axis=0)
    pair = jnp.concatenate([mine, lax.ppermute(mine, "expert", far)], axis=0)
    rows_f = jnp.concatenate([pair, lax.ppermute(pair, "expert", near)], axis=0)

    xb = x_bwd[0].astype(jnp.float32)
    r_b = rms_scale(xb)
    small = jnp.concatenate(
        [
            slots_of(route_bwd[0, :, 0]).astype(jnp.float32),
            r_b[:, 0],
            gate_bwd[0, :, 0].astype(jnp.float32) / 256.0,
        ]
    )
    small = lax.all_to_all(
        jnp.broadcast_to(small[None, None, :], (ring, 1, 3 * tokens)),
        "expert",
        split_axis=0,
        concat_axis=0,
        tiled=True,
        axis_index_groups=same_core,
    )[:, 0]
    slots_b, rs_b, scales_b = [
        small[:, i * tokens : (i + 1) * tokens].reshape(ring * tokens) for i in range(3)
    ]
    slots_b = slots_b.astype(jnp.int32)

    gate_o = lax.ppermute(w_gate[0], "expert", swap)
    up_o = lax.ppermute(w_up[0], "expert", swap)
    down_o = lax.ppermute(w_down[0], "expert", swap)
    last_f = passed_along(x_fwd[0], "section", 1).astype(jnp.float32)
    last_b = passed_along(sent, "section", -1).astype(jnp.float32)
    last_gain = passed_along(norm_gain, "section", -1)
    whole = jnp.concatenate([route_fwd[0, :, 0], gate_fwd[0, :, 0]])[None, :]
    whole = passed_along(whole, "section", 1)[0]
    last_put_f = pick_rows(whole[:tokens], me_group)
    last_scale_f = whole[tokens:, None].astype(jnp.float32) / 256.0
    last_put_b = pick_rows(passed_along(route_bwd[0, :, 0][None, :], "section", -1)[0], me_group)

    w_in = jnp.concatenate([w_gate[0], gate_o, w_up[0], up_o], axis=1)
    w_gained = (w_in.astype(jnp.float32) * gain[:, None]).astype(jnp.bfloat16)
    w_dn = jnp.concatenate([w_down[0], down_o], axis=0)
    hid = w_dn.shape[0]
    dn_stack = jnp.concatenate([w_dn[:, :half], w_dn[:, half:]], axis=0)
    in_stack = jnp.concatenate([w_in[:half], w_in[half:]], axis=1)
    w_gained, w_dn, in_stack, dn_stack = lax.optimization_barrier(
        (w_gained, w_dn, in_stack, dn_stack)
    )

    pre_f = dot(rows_f, in_stack, ((1,), (0,))).reshape(ring, unit, 4 * hid)
    pre_f = pre_f[:, :CAP, : 2 * hid] + pre_f[:, CAP:, 2 * hid :]
    act = (jax.nn.silu(pre_f[..., :hid]) * pre_f[..., hid:]).astype(jnp.bfloat16)
    lower = jnp.pad(act, ((0, 0), (0, CAP), (0, 0)))
    upper = jnp.pad(act, ((0, 0), (CAP, 0), (0, 0)))
    act = jnp.concatenate([lower, upper], axis=2).reshape(ring * unit, 2 * hid)
    part_f = dot(act, dn_stack, ((1,), (0,))).astype(jnp.bfloat16)
    pair = add(part_f[: 2 * part], lax.ppermute(part_f[2 * part :], "expert", near))
    total_f = add(pair[:part], lax.ppermute(pair[part:], "expert", far))
    got_b, total_f = lax.optimization_barrier((got_b, total_f))
    table_f = [
        to_section(total_f[k * unit : (k + 1) * unit], sections, count, 1, -side * k, ring)
        for k in range(EXPERTS)
    ]

    pre_b = dot(got_b[:, :width], w_gained, ((1,), (0,))) * rs_b[:, None]
    d_act = dot(got_b[:, width:], w_dn, ((1,), (1,))) * scales_b[:, None]
    gate, up = pre_b[:, :hid], pre_b[:, hid:]
    sig = jax.nn.sigmoid(gate)
    d_gate = (d_act * up * sig * (1.0 + gate * (1.0 - sig))).astype(jnp.bfloat16)
    d_up = (d_act * gate * sig).astype(jnp.bfloat16)
    hidden_b = jnp.concatenate([d_gate, d_up], axis=1)
    places = packers(slots_b, me_group, me_place, tokens, side)
    parts = [dot(p, hidden_b, ((1,), (0,))).astype(jnp.bfloat16) for p in places]
    part_b = dot(jnp.concatenate(parts, axis=1), in_stack, ((1,), (1,))).astype(jnp.bfloat16)
    total_b = part_b[:part].astype(jnp.float32)
    for k in range(1, side):
        hop = in_group(count, side, lambda j: (j - k) % side)
        back = lax.ppermute(part_b[k * part : (k + 1) * part], "expert", hop)
        total_b = total_b + back.astype(jnp.float32)
    total_b = total_b.astype(jnp.bfloat16)
    table_b = [
        to_section(total_b[k * unit : (k + 1) * unit], sections, count, -1, -side * k, ring)
        for k in range(EXPERTS)
    ]

    moe_f = dot(last_put_f, jnp.concatenate(table_f, axis=0), ((0,), (0,)))
    moe_f = jnp.concatenate([moe_f[:tokens], moe_f[tokens:]], axis=1)
    y_next = (last_f + last_scale_f * moe_f).astype(jnp.bfloat16)

    d_normed = dot(last_put_b, jnp.concatenate(table_b, axis=0), ((0,), (0,)))
    d_normed = jnp.concatenate([d_normed[:tokens], d_normed[tokens:]], axis=1)
    last_x, last_g = last_b[:, :width], last_b[:, width:]
    r = rms_scale(last_x)
    weighted = d_normed * last_gain
    inner = jnp.mean(last_x * weighted, axis=-1, keepdims=True)
    dx_prev = (last_g + (r * weighted - last_x * r * r * r * inner)).astype(jnp.bfloat16)
    return (y_next[None], dx_prev[None])


def solution(mesh):
    in_specs = (
        P("section", "expert", None),
        P("section", "expert", None),
        P("section", "expert", None),
        P("section", None),
        P("section", None, "expert"),
        P("section", None, "expert"),
        P("section", "expert", None),
        P("section", "expert", None),
        P("section", "expert", None),
        P("section", "expert", None),
        P("section", "expert", None),
    )
    out_specs = (P("section", "expert", None), P("section", "expert", None))
    return jax.shard_map(
        per_device, mesh=mesh, in_specs=in_specs, out_specs=out_specs, check_vma=False
    )
```

```python
import jax
import jax.numpy as jnp
from jax import lax
from jax.sharding import PartitionSpec as P

EXPERTS = 4
CAP = 12
EPSILON = 1e-06


def passed_along(value, axis, steps):
    count = lax.axis_size(axis)
    pairs = [(source, (source + steps) % count) for source in range(count)]
    return lax.ppermute(value, axis, pairs)


def rms_scale(values):
    return lax.rsqrt(jnp.mean(values * values, axis=-1, keepdims=True) + EPSILON)


def dot(a, b, dims):
    return lax.dot_general(a, b, (dims, ((), ())), preferred_element_type=jnp.float32)


def slots_of(route):
    onehot = (route[:, None] == jnp.arange(EXPERTS, dtype=jnp.int32)[None, :]).astype(jnp.int32)
    rank = jnp.sum(jnp.cumsum(onehot, axis=0) * onehot, axis=1) - 1
    return route * CAP + rank


def half_places(slot):
    expert, rank = slot // CAP, slot % CAP
    base = expert * (2 * CAP) + rank
    return [base + h * CAP for h in range(2)]


def pick_back(table, slot):
    rows = table.reshape(-1, table.shape[-1])
    count = rows.shape[0]
    halves = []
    for place in half_places(slot):
        pick = (place[:, None] == jnp.arange(count, dtype=jnp.int32)[None, :]).astype(jnp.bfloat16)
        halves.append(dot(pick, rows, ((1,), (0,))))
    return jnp.concatenate(halves, axis=1)


def group_to_section(value, sections, count, side, steps, hop):
    pairs = []
    for s in range(sections):
        for d in range(count):
            chip, core = d // 2, d % 2
            chip = chip // side * side + (chip % side + hop) % side
            pairs.append((s * count + d, (s + steps) % sections * count + 2 * chip + core))
    return lax.ppermute(value, ("section", "expert"), pairs)


def packers(slots, me_expert, first_place, tokens, side, turn):
    count = slots.shape[0]
    sources = count // tokens
    groups = sources // side
    expert, rank = slots // CAP, slots % CAP
    source = jnp.arange(count, dtype=jnp.int32) // tokens
    place = (turn * (source % side - first_place)) % side
    base = (place * groups + source // side) * (2 * CAP) + rank
    base = jnp.where(expert == me_expert, base, -2 * CAP)
    row = jnp.arange(sources * 2 * CAP, dtype=jnp.int32)[:, None]
    return [(base[None, :] + h * CAP == row).astype(jnp.bfloat16) for h in range(2)]


def pack(places, hidden):
    parts = [dot(place, hidden, ((1,), (0,))).astype(jnp.bfloat16) for place in places]
    return jnp.concatenate(parts, axis=1)


def across_groups(rows, across):
    return lax.all_to_all(
        rows.reshape(EXPERTS, 2 * CAP, rows.shape[1]),
        "expert",
        split_axis=0,
        concat_axis=0,
        tiled=True,
        axis_index_groups=across,
    )


def per_device(
    x_fwd,
    x_bwd,
    grad_out,
    norm_gain,
    w_gate,
    w_up,
    w_down,
    route_fwd,
    gate_fwd,
    route_bwd,
    gate_bwd,
):
    sections = lax.axis_size("section")
    count = lax.axis_size("expert")
    ring = count // 2
    side = ring // EXPERTS
    same_core = [[2 * z + c for z in range(ring)] for c in range(2)]
    within = [[2 * (side * g + j) + c for j in range(side)] for g in range(EXPERTS) for c in range(2)]
    across = [[2 * (side * g + j) + c for g in range(EXPERTS)] for j in range(side) for c in range(2)]
    swap = [(i, i ^ 1) for i in range(count)]
    index = lax.axis_index("expert")
    me_expert = index // (2 * side)
    me_place = (index // 2) % side

    gain = norm_gain[0]
    tokens, width = x_fwd.shape[1:]
    half = width // 2
    sent_b = jnp.concatenate([x_bwd[0], grad_out[0]], axis=1)
    sent = jnp.concatenate([x_fwd[0], x_bwd[0], grad_out[0]], axis=1)
    got = lax.all_gather(sent, "expert", axis=0, tiled=True, axis_index_groups=same_core)

    xf = x_fwd[0].astype(jnp.float32)
    xb = x_bwd[0].astype(jnp.float32)
    scale_f = gate_fwd[0].astype(jnp.float32) / 256.0
    slot_f = slots_of(route_fwd[0, :, 0])
    slot_b = slots_of(route_bwd[0, :, 0])
    small = jnp.concatenate(
        [
            slot_f.astype(jnp.float32),
            slot_b.astype(jnp.float32),
            rms_scale(xf)[:, 0],
            rms_scale(xb)[:, 0],
            gate_bwd[0, :, 0].astype(jnp.float32) / 256.0,
        ]
    )
    small = lax.all_to_all(
        jnp.broadcast_to(small[None, None, :], (ring, 1, 5 * tokens)),
        "expert",
        split_axis=0,
        concat_axis=0,
        tiled=True,
        axis_index_groups=same_core,
    )[:, 0]
    slots_f, slots_b, rs_f, rs_b, scales_b = [
        small[:, i * tokens : (i + 1) * tokens].reshape(ring * tokens) for i in range(5)
    ]
    slots_f = slots_f.astype(jnp.int32)
    slots_b = slots_b.astype(jnp.int32)
    places_f = packers(slots_f, me_expert, 0, tokens, side, 1)
    places_b = packers(slots_b, me_expert, me_place, tokens, side, -1)

    gate_o = lax.ppermute(w_gate[0], "expert", swap)
    up_o = lax.ppermute(w_up[0], "expert", swap)
    down_o = lax.ppermute(w_down[0], "expert", swap)
    w_in = jnp.concatenate([w_gate[0], gate_o, w_up[0], up_o], axis=1)
    w_gained = (w_in.astype(jnp.float32) * gain[:, None]).astype(jnp.bfloat16)
    w_dn = jnp.concatenate([w_down[0], down_o], axis=0)
    hid = w_dn.shape[0]
    dn_stack = jnp.concatenate([w_dn[:, :half], w_dn[:, half:]], axis=0)
    in_stack = jnp.concatenate([w_in[:half], w_in[half:]], axis=1)
    w_gained, w_dn, in_stack, dn_stack = lax.optimization_barrier(
        (w_gained, w_dn, in_stack, dn_stack)
    )

    last_b = passed_along(sent_b, "section", -1).astype(jnp.float32)
    last_gain = passed_along(norm_gain, "section", -1)
    last_slot = passed_along(slot_b[None, :], "section", -1)[0]

    pre_f = dot(got[:, :width], w_gained, ((1,), (0,))) * rs_f[:, None]
    act = (jax.nn.silu(pre_f[:, :hid]) * pre_f[:, hid:]).astype(jnp.bfloat16)
    part_f = dot(pack(places_f, act), dn_stack, ((1,), (0,))).astype(jnp.bfloat16)
    got, part_f = lax.optimization_barrier((got, part_f))
    total_f = lax.psum_scatter(
        part_f, "expert", scatter_dimension=0, tiled=True, axis_index_groups=within
    )

    pre_b = dot(got[:, width : 2 * width], w_gained, ((1,), (0,))) * rs_b[:, None]
    d_act = dot(got[:, 2 * width :], w_dn, ((1,), (1,))) * scales_b[:, None]
    gate, up = pre_b[:, :hid], pre_b[:, hid:]
    sig = jax.nn.sigmoid(gate)
    d_gate = (d_act * up * sig * (1.0 + gate * (1.0 - sig))).astype(jnp.bfloat16)
    d_up = (d_act * gate * sig).astype(jnp.bfloat16)
    hidden_b = pack(places_b, jnp.concatenate([d_gate, d_up], axis=1))
    part_b = dot(hidden_b, in_stack, ((1,), (1,))).astype(jnp.bfloat16)
    rows = part_b.shape[0] // side
    total_b = sum(
        group_to_section(
            part_b[k * rows : (k + 1) * rows], sections, count, side, -1, -k
        ).astype(jnp.float32)
        for k in range(side)
    ).astype(jnp.bfloat16)

    table_f = across_groups(total_f, across)
    seen = table_f[0, 0, 0].astype(jnp.float32)
    total_b = jnp.where((seen > 1.0) & (seen < -1.0), 0, total_b)
    moe_f = pick_back(table_f, slot_f)
    y = (xf + scale_f * moe_f).astype(jnp.bfloat16)
    y_next = passed_along(y, "section", 1)

    d_normed = pick_back(across_groups(total_b, across), last_slot)
    last_x, last_g = last_b[:, :width], last_b[:, width:]
    r = rms_scale(last_x)
    weighted = d_normed * last_gain
    inner = jnp.mean(last_x * weighted, axis=-1, keepdims=True)
    dx_prev = (last_g + (r * weighted - last_x * r * r * r * inner)).astype(jnp.bfloat16)
    return (y_next[None], dx_prev[None])


def solution(mesh):
    in_specs = (
        P("section", "expert", None),
        P("section", "expert", None),
        P("section", "expert", None),
        P("section", None),
        P("section", None, "expert"),
        P("section", None, "expert"),
        P("section", "expert", None),
        P("section", "expert", None),
        P("section", "expert", None),
        P("section", "expert", None),
        P("section", "expert", None),
    )
    out_specs = (P("section", "expert", None), P("section", "expert", None))
    return jax.shard_map(
        per_device, mesh=mesh, in_specs=in_specs, out_specs=out_specs, check_vma=False
    )
```

```python
import jax
import jax.numpy as jnp
from jax import lax
from jax.sharding import PartitionSpec as P

EXPERTS = 4
CAP = 12
EPSILON = 1e-06


def passed_along(value, axis, steps):
    count = lax.axis_size(axis)
    pairs = [(source, (source + steps) % count) for source in range(count)]
    return lax.ppermute(value, axis, pairs)


def rms_scale(values):
    return lax.rsqrt(jnp.mean(values * values, axis=-1, keepdims=True) + EPSILON)


def dot(a, b, dims):
    return lax.dot_general(a, b, (dims, ((), ())), preferred_element_type=jnp.float32)


def slots_of(route):
    onehot = (route[:, None] == jnp.arange(EXPERTS, dtype=jnp.int32)[None, :]).astype(jnp.int32)
    rank = jnp.sum(jnp.cumsum(onehot, axis=0) * onehot, axis=1) - 1
    return route * CAP + rank


def half_places(slot):
    expert, rank = slot // CAP, slot % CAP
    base = expert * (2 * CAP) + rank
    return [base + h * CAP for h in range(2)]


def pick_back(table, slot):
    rows = table.reshape(-1, table.shape[-1])
    count = rows.shape[0]
    halves = []
    for place in half_places(slot):
        pick = (place[:, None] == jnp.arange(count, dtype=jnp.int32)[None, :]).astype(jnp.bfloat16)
        halves.append(dot(pick, rows, ((1,), (0,))))
    return jnp.concatenate(halves, axis=1)


def to_section(value, sections, count, steps, hop, chips):
    pairs = []
    for s in range(sections):
        for d in range(count):
            chip = (d // 2 + hop) % chips
            pairs.append((s * count + d, (s + steps) % sections * count + 2 * chip + d % 2))
    return lax.ppermute(value, ("section", "expert"), pairs)


def pick_rows(route, me_group):
    slot = slots_of(route)
    place = (slot // CAP - me_group) % EXPERTS * (2 * CAP) + slot % CAP
    want = jnp.concatenate([place, place + CAP])
    row = jnp.arange(EXPERTS * 2 * CAP, dtype=jnp.int32)[:, None]
    return (row == want[None, :]).astype(jnp.bfloat16)


def group_to_section(value, sections, count, side, steps, hop):
    pairs = []
    for s in range(sections):
        for d in range(count):
            chip, core = d // 2, d % 2
            chip = chip // side * side + (chip % side + hop) % side
            pairs.append((s * count + d, (s + steps) % sections * count + 2 * chip + core))
    return lax.ppermute(value, ("section", "expert"), pairs)


def packers(slots, me_expert, first_place, tokens, side, turn, near_first=False):
    count = slots.shape[0]
    sources = count // tokens
    groups = sources // side
    expert, rank = slots // CAP, slots % CAP
    source = jnp.arange(count, dtype=jnp.int32) // tokens
    place = (turn * (source % side - first_place)) % side
    group = source // side
    if near_first:
        group = (me_expert - group) % groups
    base = (place * groups + group) * (2 * CAP) + rank
    base = jnp.where(expert == me_expert, base, -2 * CAP)
    row = jnp.arange(sources * 2 * CAP, dtype=jnp.int32)[:, None]
    return [(base[None, :] + h * CAP == row).astype(jnp.bfloat16) for h in range(2)]


def pack(places, hidden):
    parts = [dot(place, hidden, ((1,), (0,))).astype(jnp.bfloat16) for place in places]
    return jnp.concatenate(parts, axis=1)


def across_groups(rows, across):
    return lax.all_to_all(
        rows.reshape(EXPERTS, 2 * CAP, rows.shape[1]),
        "expert",
        split_axis=0,
        concat_axis=0,
        tiled=True,
        axis_index_groups=across,
    )


def per_device(
    x_fwd,
    x_bwd,
    grad_out,
    norm_gain,
    w_gate,
    w_up,
    w_down,
    route_fwd,
    gate_fwd,
    route_bwd,
    gate_bwd,
):
    sections = lax.axis_size("section")
    count = lax.axis_size("expert")
    ring = count // 2
    side = ring // EXPERTS
    same_core = [[2 * z + c for z in range(ring)] for c in range(2)]
    within = [[2 * (side * g + j) + c for j in range(side)] for g in range(EXPERTS) for c in range(2)]
    across = [[2 * (side * g + j) + c for g in range(EXPERTS)] for j in range(side) for c in range(2)]
    swap = [(i, i ^ 1) for i in range(count)]
    index = lax.axis_index("expert")
    me_expert = index // (2 * side)
    me_place = (index // 2) % side

    gain = norm_gain[0]
    tokens, width = x_fwd.shape[1:]
    half = width // 2
    sent_b = jnp.concatenate([x_bwd[0], grad_out[0]], axis=1)
    sent = jnp.concatenate([x_fwd[0], x_bwd[0], grad_out[0]], axis=1)
    got = lax.all_gather(sent, "expert", axis=0, tiled=True, axis_index_groups=same_core)

    xf = x_fwd[0].astype(jnp.float32)
    xb = x_bwd[0].astype(jnp.float32)
    slot_f = slots_of(route_fwd[0, :, 0])
    slot_b = slots_of(route_bwd[0, :, 0])
    small = jnp.concatenate(
        [
            slot_f.astype(jnp.float32),
            slot_b.astype(jnp.float32),
            rms_scale(xf)[:, 0],
            rms_scale(xb)[:, 0],
            gate_bwd[0, :, 0].astype(jnp.float32) / 256.0,
        ]
    )
    small = lax.all_to_all(
        jnp.broadcast_to(small[None, None, :], (ring, 1, 5 * tokens)),
        "expert",
        split_axis=0,
        concat_axis=0,
        tiled=True,
        axis_index_groups=same_core,
    )[:, 0]
    slots_f, slots_b, rs_f, rs_b, scales_b = [
        small[:, i * tokens : (i + 1) * tokens].reshape(ring * tokens) for i in range(5)
    ]
    slots_f = slots_f.astype(jnp.int32)
    slots_b = slots_b.astype(jnp.int32)
    places_f = packers(slots_f, me_expert, 0, tokens, side, 1, near_first=True)
    places_b = packers(slots_b, me_expert, me_place, tokens, side, -1)

    gate_o = lax.ppermute(w_gate[0], "expert", swap)
    up_o = lax.ppermute(w_up[0], "expert", swap)
    down_o = lax.ppermute(w_down[0], "expert", swap)
    w_in = jnp.concatenate([w_gate[0], gate_o, w_up[0], up_o], axis=1)
    w_gained = (w_in.astype(jnp.float32) * gain[:, None]).astype(jnp.bfloat16)
    w_dn = jnp.concatenate([w_down[0], down_o], axis=0)
    hid = w_dn.shape[0]
    dn_stack = jnp.concatenate([w_dn[:, :half], w_dn[:, half:]], axis=0)
    in_stack = jnp.concatenate([w_in[:half], w_in[half:]], axis=1)
    last_f = passed_along(x_fwd[0], "section", 1)
    last_b = passed_along(sent_b, "section", -1)
    last_gain = passed_along(norm_gain, "section", -1)
    whole = jnp.concatenate([route_fwd[0, :, 0], gate_fwd[0, :, 0]])[None, :]
    whole = passed_along(whole, "section", 1)[0]
    last_slot = passed_along(slot_b[None, :], "section", -1)[0]
    seen = last_f[0, 0] + last_b[0, 0] + last_gain[0, 0] + (whole[0] + last_slot[0])
    seen = seen.astype(jnp.float32)
    dn_stack = jnp.where((seen > 1.0) & (seen < -1.0), 0, dn_stack)
    w_gained, w_dn, in_stack, dn_stack = lax.optimization_barrier(
        (w_gained, w_dn, in_stack, dn_stack)
    )
    last_put = pick_rows(whole[:tokens], me_expert)
    last_scale = whole[tokens:, None].astype(jnp.float32) / 256.0

    pre_f = dot(got[:, :width], w_gained, ((1,), (0,))) * rs_f[:, None]
    act = (jax.nn.silu(pre_f[:, :hid]) * pre_f[:, hid:]).astype(jnp.bfloat16)
    part_f = dot(pack(places_f, act), dn_stack, ((1,), (0,))).astype(jnp.bfloat16)
    got, part_f = lax.optimization_barrier((got, part_f))
    total_f = lax.psum_scatter(
        part_f, "expert", scatter_dimension=0, tiled=True, axis_index_groups=within
    )

    pre_b = dot(got[:, width : 2 * width], w_gained, ((1,), (0,))) * rs_b[:, None]
    d_act = dot(got[:, 2 * width :], w_dn, ((1,), (1,))) * scales_b[:, None]
    gate, up = pre_b[:, :hid], pre_b[:, hid:]
    sig = jax.nn.sigmoid(gate)
    d_gate = (d_act * up * sig * (1.0 + gate * (1.0 - sig))).astype(jnp.bfloat16)
    d_up = (d_act * gate * sig).astype(jnp.bfloat16)
    hidden_b = pack(places_b, jnp.concatenate([d_gate, d_up], axis=1))
    part_b = dot(hidden_b, in_stack, ((1,), (1,))).astype(jnp.bfloat16)
    rows = part_b.shape[0] // side
    total_b = sum(
        group_to_section(
            part_b[k * rows : (k + 1) * rows], sections, count, side, -1, -k
        ).astype(jnp.float32)
        for k in range(side)
    ).astype(jnp.bfloat16)

    seen = total_f[0, 0].astype(jnp.float32)
    total_b = jnp.where((seen > 1.0) & (seen < -1.0), 0, total_b)
    unit = 2 * CAP
    table_f = [
        to_section(total_f[k * unit : (k + 1) * unit], sections, count, 1, -side * k, ring)
        for k in range(EXPERTS)
    ]
    moe_f = dot(last_put, jnp.concatenate(table_f, axis=0), ((0,), (0,)))
    moe_f = jnp.concatenate([moe_f[:tokens], moe_f[tokens:]], axis=1)
    y_next = (last_f.astype(jnp.float32) + last_scale * moe_f).astype(jnp.bfloat16)

    d_normed = pick_back(across_groups(total_b, across), last_slot)
    last_b = last_b.astype(jnp.float32)
    last_x, last_g = last_b[:, :width], last_b[:, width:]
    r = rms_scale(last_x)
    weighted = d_normed * last_gain
    inner = jnp.mean(last_x * weighted, axis=-1, keepdims=True)
    dx_prev = (last_g + (r * weighted - last_x * r * r * r * inner)).astype(jnp.bfloat16)
    return (y_next[None], dx_prev[None])


def solution(mesh):
    in_specs = (
        P("section", "expert", None),
        P("section", "expert", None),
        P("section", "expert", None),
        P("section", None),
        P("section", None, "expert"),
        P("section", None, "expert"),
        P("section", "expert", None),
        P("section", "expert", None),
        P("section", "expert", None),
        P("section", "expert", None),
        P("section", "expert", None),
    )
    out_specs = (P("section", "expert", None), P("section", "expert", None))
    return jax.shard_map(
        per_device, mesh=mesh, in_specs=in_specs, out_specs=out_specs, check_vma=False
    )
```

```python
import jax
import jax.numpy as jnp
from jax import lax
from jax.sharding import PartitionSpec as P

EXPERTS = 4
CAP = 12
EPSILON = 1e-06


def passed_along(value, axis, steps):
    count = lax.axis_size(axis)
    pairs = [(source, (source + steps) % count) for source in range(count)]
    return lax.ppermute(value, axis, pairs)


def rms_scale(values):
    return lax.rsqrt(jnp.mean(values * values, axis=-1, keepdims=True) + EPSILON)


def dot(a, b, dims):
    return lax.dot_general(a, b, (dims, ((), ())), preferred_element_type=jnp.float32)


def slots_of(route):
    onehot = (route[:, None] == jnp.arange(EXPERTS, dtype=jnp.int32)[None, :]).astype(jnp.int32)
    rank = jnp.sum(jnp.cumsum(onehot, axis=0) * onehot, axis=1) - 1
    return route * CAP + rank


def half_places(slot):
    expert, rank = slot // CAP, slot % CAP
    base = expert * (2 * CAP) + rank
    return [base + h * CAP for h in range(2)]


def pick_back(table, slot):
    rows = table.reshape(-1, table.shape[-1])
    count = rows.shape[0]
    halves = []
    for place in half_places(slot):
        pick = (place[:, None] == jnp.arange(count, dtype=jnp.int32)[None, :]).astype(jnp.bfloat16)
        halves.append(dot(pick, rows, ((1,), (0,))))
    return jnp.concatenate(halves, axis=1)


def group_to_section(value, sections, count, side, steps, hop):
    pairs = []
    for s in range(sections):
        for d in range(count):
            chip, core = d // 2, d % 2
            chip = chip // side * side + (chip % side + hop) % side
            pairs.append((s * count + d, (s + steps) % sections * count + 2 * chip + core))
    return lax.ppermute(value, ("section", "expert"), pairs)


def packers(slots, me_expert, first_place, tokens, side, turn):
    count = slots.shape[0]
    sources = count // tokens
    groups = sources // side
    expert, rank = slots // CAP, slots % CAP
    source = jnp.arange(count, dtype=jnp.int32) // tokens
    place = (turn * (source % side - first_place)) % side
    base = (place * groups + source // side) * (2 * CAP) + rank
    base = jnp.where(expert == me_expert, base, -2 * CAP)
    row = jnp.arange(sources * 2 * CAP, dtype=jnp.int32)[:, None]
    return [(base[None, :] + h * CAP == row).astype(jnp.bfloat16) for h in range(2)]


def pack(places, hidden):
    parts = [dot(place, hidden, ((1,), (0,))).astype(jnp.bfloat16) for place in places]
    return jnp.concatenate(parts, axis=1)


def across_groups(parts, across):
    blocks = [rows.reshape(EXPERTS, 2 * CAP, rows.shape[1]) for rows in parts]
    table = lax.all_to_all(
        jnp.concatenate(blocks, axis=1),
        "expert",
        split_axis=0,
        concat_axis=0,
        tiled=True,
        axis_index_groups=across,
    )
    return [table[:, i * 2 * CAP : (i + 1) * 2 * CAP] for i in range(len(parts))]


def per_device(
    x_fwd,
    x_bwd,
    grad_out,
    norm_gain,
    w_gate,
    w_up,
    w_down,
    route_fwd,
    gate_fwd,
    route_bwd,
    gate_bwd,
):
    sections = lax.axis_size("section")
    count = lax.axis_size("expert")
    ring = count // 2
    side = ring // EXPERTS
    same_core = [[2 * z + c for z in range(ring)] for c in range(2)]
    within = [[2 * (side * g + j) + c for j in range(side)] for g in range(EXPERTS) for c in range(2)]
    across = [[2 * (side * g + j) + c for g in range(EXPERTS)] for j in range(side) for c in range(2)]
    swap = [(i, i ^ 1) for i in range(count)]
    index = lax.axis_index("expert")
    me_expert = index // (2 * side)
    me_place = (index // 2) % side

    gain = norm_gain[0]
    tokens, width = x_fwd.shape[1:]
    half = width // 2
    sent_b = jnp.concatenate([x_bwd[0], grad_out[0]], axis=1)
    sent = jnp.concatenate([x_fwd[0], x_bwd[0], grad_out[0]], axis=1)
    got = lax.all_gather(sent, "expert", axis=0, tiled=True, axis_index_groups=same_core)

    xf = x_fwd[0].astype(jnp.float32)
    xb = x_bwd[0].astype(jnp.float32)
    slot_f = slots_of(route_fwd[0, :, 0])
    slot_b = slots_of(route_bwd[0, :, 0])
    small = jnp.concatenate(
        [
            slot_f.astype(jnp.float32),
            slot_b.astype(jnp.float32),
            rms_scale(xf)[:, 0],
            rms_scale(xb)[:, 0],
            gate_bwd[0, :, 0].astype(jnp.float32) / 256.0,
        ]
    )
    small = lax.all_to_all(
        jnp.broadcast_to(small[None, None, :], (ring, 1, 5 * tokens)),
        "expert",
        split_axis=0,
        concat_axis=0,
        tiled=True,
        axis_index_groups=same_core,
    )[:, 0]
    slots_f, slots_b, rs_f, rs_b, scales_b = [
        small[:, i * tokens : (i + 1) * tokens].reshape(ring * tokens) for i in range(5)
    ]
    slots_f = slots_f.astype(jnp.int32)
    slots_b = slots_b.astype(jnp.int32)
    places_f = packers(slots_f, me_expert, 0, tokens, side, 1)
    places_b = packers(slots_b, me_expert, me_place, tokens, side, -1)

    gate_o = lax.ppermute(w_gate[0], "expert", swap)
    up_o = lax.ppermute(w_up[0], "expert", swap)
    down_o = lax.ppermute(w_down[0], "expert", swap)
    w_in = jnp.concatenate([w_gate[0], gate_o, w_up[0], up_o], axis=1)
    w_gained = (w_in.astype(jnp.float32) * gain[:, None]).astype(jnp.bfloat16)
    w_dn = jnp.concatenate([w_down[0], down_o], axis=0)
    hid = w_dn.shape[0]
    dn_stack = jnp.concatenate([w_dn[:, :half], w_dn[:, half:]], axis=0)
    in_stack = jnp.concatenate([w_in[:half], w_in[half:]], axis=1)
    last_b = passed_along(sent_b, "section", -1)
    last_gain = passed_along(norm_gain, "section", -1)
    last_slot = passed_along(slot_b[None, :], "section", -1)[0]
    seen = last_b[0, 0] + last_gain[0, 0] + last_slot[0]
    seen = seen.astype(jnp.float32)
    dn_stack = jnp.where((seen > 1.0) & (seen < -1.0), 0, dn_stack)
    w_gained, w_dn, in_stack, dn_stack = lax.optimization_barrier(
        (w_gained, w_dn, in_stack, dn_stack)
    )

    pre_f = dot(got[:, :width], w_gained, ((1,), (0,))) * rs_f[:, None]
    act = (jax.nn.silu(pre_f[:, :hid]) * pre_f[:, hid:]).astype(jnp.bfloat16)
    part_f = dot(pack(places_f, act), dn_stack, ((1,), (0,))).astype(jnp.bfloat16)
    got, part_f = lax.optimization_barrier((got, part_f))
    total_f = lax.psum_scatter(
        part_f, "expert", scatter_dimension=0, tiled=True, axis_index_groups=within
    )

    pre_b = dot(got[:, width : 2 * width], w_gained, ((1,), (0,))) * rs_b[:, None]
    d_act = dot(got[:, 2 * width :], w_dn, ((1,), (1,))) * scales_b[:, None]
    gate, up = pre_b[:, :hid], pre_b[:, hid:]
    sig = jax.nn.sigmoid(gate)
    d_gate = (d_act * up * sig * (1.0 + gate * (1.0 - sig))).astype(jnp.bfloat16)
    d_up = (d_act * gate * sig).astype(jnp.bfloat16)
    hidden_b = pack(places_b, jnp.concatenate([d_gate, d_up], axis=1))
    part_b = dot(hidden_b, in_stack, ((1,), (1,))).astype(jnp.bfloat16)
    rows = part_b.shape[0] // side
    total_b = sum(
        group_to_section(
            part_b[k * rows : (k + 1) * rows], sections, count, side, -1, -k
        ).astype(jnp.float32)
        for k in range(side)
    ).astype(jnp.bfloat16)

    table_f, table_b = across_groups([total_f, total_b], across)
    moe_f = pick_back(table_f, slot_f)
    scale_f = gate_fwd[0].astype(jnp.float32) / 256.0
    y_next = passed_along((xf + scale_f * moe_f).astype(jnp.bfloat16), "section", 1)

    last_b = last_b.astype(jnp.float32)
    d_normed = pick_back(table_b, last_slot)
    last_x, last_g = last_b[:, :width], last_b[:, width:]
    r = rms_scale(last_x)
    weighted = d_normed * last_gain
    inner = jnp.mean(last_x * weighted, axis=-1, keepdims=True)
    dx_prev = (last_g + (r * weighted - last_x * r * r * r * inner)).astype(jnp.bfloat16)
    return (y_next[None], dx_prev[None])


def solution(mesh):
    in_specs = (
        P("section", "expert", None),
        P("section", "expert", None),
        P("section", "expert", None),
        P("section", None),
        P("section", None, "expert"),
        P("section", None, "expert"),
        P("section", "expert", None),
        P("section", "expert", None),
        P("section", "expert", None),
        P("section", "expert", None),
        P("section", "expert", None),
    )
    out_specs = (P("section", "expert", None), P("section", "expert", None))
    return jax.shard_map(
        per_device, mesh=mesh, in_specs=in_specs, out_specs=out_specs, check_vma=False
    )
```

```python
import jax
import jax.numpy as jnp
from jax import lax
from jax.sharding import PartitionSpec as P

EXPERTS = 4
CAP = 12
EPSILON = 1e-06


def passed_along(value, axis, steps):
    count = lax.axis_size(axis)
    pairs = [(source, (source + steps) % count) for source in range(count)]
    return lax.ppermute(value, axis, pairs)


def rms_scale(values):
    return lax.rsqrt(jnp.mean(values * values, axis=-1, keepdims=True) + EPSILON)


def dot(a, b, dims):
    return lax.dot_general(a, b, (dims, ((), ())), preferred_element_type=jnp.float32)


def slots_of(route):
    onehot = (route[:, None] == jnp.arange(EXPERTS, dtype=jnp.int32)[None, :]).astype(jnp.int32)
    rank = jnp.sum(jnp.cumsum(onehot, axis=0) * onehot, axis=1) - 1
    return route * CAP + rank


def half_places(slot):
    expert, rank = slot // CAP, slot % CAP
    base = expert * (2 * CAP) + rank
    return [base + h * CAP for h in range(2)]


def pick_back(table, slot):
    rows = table.reshape(-1, table.shape[-1])
    count = rows.shape[0]
    halves = []
    for place in half_places(slot):
        pick = (place[:, None] == jnp.arange(count, dtype=jnp.int32)[None, :]).astype(jnp.bfloat16)
        halves.append(dot(pick, rows, ((1,), (0,))))
    return jnp.concatenate(halves, axis=1)


def partners(count, side, bits):
    pairs = []
    for device in range(count):
        chip, core = device // 2, device % 2
        pairs.append((device, 2 * (chip // side * side + (chip % side ^ bits)) + core))
    return pairs


def packers(slots, me_expert, me_place, tokens, side):
    count = slots.shape[0]
    sources = count // tokens
    groups = sources // side
    expert, rank = slots // CAP, slots % CAP
    source = jnp.arange(count, dtype=jnp.int32) // tokens
    differs = source % side ^ me_place
    block = differs // 2 + differs % 2 * 2
    base = block * (groups * 2 * CAP) + (source // side) * (2 * CAP) + rank
    base = jnp.where(expert == me_expert, base, -2 * CAP)
    row = jnp.arange(sources * 2 * CAP, dtype=jnp.int32)[:, None]
    return [(base[None, :] + h * CAP == row).astype(jnp.bfloat16) for h in range(2)]


def join_group(partial, count, side):
    rows, width = partial.shape
    blocks = partial.astype(jnp.bfloat16)
    for part, bits in ((rows // 2, 1), (rows // 4, 2)):
        got = lax.ppermute(blocks[part:], "expert", partners(count, side, bits))
        total = blocks[:part].astype(jnp.float32) + got.astype(jnp.float32)
        blocks = total.astype(jnp.bfloat16)
    return blocks.reshape(EXPERTS, 2 * CAP, width)


def across_groups(blocks, across):
    return lax.all_to_all(
        blocks, "expert", split_axis=0, concat_axis=0, tiled=True, axis_index_groups=across
    )


def per_device(
    x_fwd,
    x_bwd,
    grad_out,
    norm_gain,
    w_gate,
    w_up,
    w_down,
    route_fwd,
    gate_fwd,
    route_bwd,
    gate_bwd,
):
    count = lax.axis_size("expert")
    ring = count // 2
    side = ring // EXPERTS
    same_core = [[2 * z + c for z in range(ring)] for c in range(2)]
    across = [[2 * (side * g + j) + c for g in range(EXPERTS)] for j in range(side) for c in range(2)]
    swap = [(i, i ^ 1) for i in range(count)]
    index = lax.axis_index("expert")
    me_expert = index // (2 * side)
    me_place = (index // 2) % side

    gain = norm_gain[0]
    tokens, width = x_fwd.shape[1:]
    half = width // 2
    sent = jnp.concatenate([x_fwd[0], x_bwd[0], grad_out[0]], axis=1)
    got = lax.all_gather(sent, "expert", axis=0, tiled=True, axis_index_groups=same_core)

    xf = x_fwd[0].astype(jnp.float32)
    xb = x_bwd[0].astype(jnp.float32)
    up32 = grad_out[0].astype(jnp.float32)
    scale_f = gate_fwd[0].astype(jnp.float32) / 256.0
    scale_b = gate_bwd[0].astype(jnp.float32) / 256.0
    r_f = rms_scale(xf)
    r_b = rms_scale(xb)
    slot_f = slots_of(route_fwd[0, :, 0])
    slot_b = slots_of(route_bwd[0, :, 0])
    small = jnp.concatenate(
        [slot_f.astype(jnp.float32), slot_b.astype(jnp.float32), r_f[:, 0], r_b[:, 0], scale_b[:, 0]]
    )
    small = lax.all_to_all(
        jnp.broadcast_to(small[None, None, :], (ring, 1, 5 * tokens)),
        "expert",
        split_axis=0,
        concat_axis=0,
        tiled=True,
        axis_index_groups=same_core,
    )[:, 0]
    slots_f, slots_b, rs_f, rs_b, scales_b = [
        small[:, i * tokens : (i + 1) * tokens].reshape(ring * tokens) for i in range(5)
    ]
    slots_f = slots_f.astype(jnp.int32)
    slots_b = slots_b.astype(jnp.int32)

    gate_o = lax.ppermute(w_gate[0], "expert", swap)
    up_o = lax.ppermute(w_up[0], "expert", swap)
    down_o = lax.ppermute(w_down[0], "expert", swap)
    w_in = jnp.concatenate([w_gate[0], gate_o, w_up[0], up_o], axis=1)
    w_gained = (w_in.astype(jnp.float32) * gain[:, None]).astype(jnp.bfloat16)
    w_dn = jnp.concatenate([w_down[0], down_o], axis=0)
    hid = w_dn.shape[0]
    in_stack = jnp.concatenate([w_in[:half], w_in[half:]], axis=1)
    w_gained, w_dn, in_stack = lax.optimization_barrier((w_gained, w_dn, in_stack))

    pre_f = dot(got[:, :width], w_gained, ((1,), (0,))) * rs_f[:, None]
    act = jax.nn.silu(pre_f[:, :hid]) * pre_f[:, hid:]
    act = jnp.where((slots_f // CAP == me_expert)[:, None], act, 0.0).astype(jnp.bfloat16)
    part_f = dot(act, w_dn, ((1,), (0,))).astype(jnp.bfloat16)
    got, part_f = lax.optimization_barrier((got, part_f))
    moe_f = lax.psum_scatter(
        part_f, "expert", scatter_dimension=0, tiled=True, axis_index_groups=same_core
    )

    pre_b = dot(got[:, width : 2 * width], w_gained, ((1,), (0,))) * rs_b[:, None]
    d_act = dot(got[:, 2 * width :], w_dn, ((1,), (1,))) * scales_b[:, None]
    gate, up = pre_b[:, :hid], pre_b[:, hid:]
    sig = jax.nn.sigmoid(gate)
    d_gate = (d_act * up * sig * (1.0 + gate * (1.0 - sig))).astype(jnp.bfloat16)
    d_up = (d_act * gate * sig).astype(jnp.bfloat16)
    hidden_b = jnp.concatenate([d_gate, d_up], axis=1)
    places = packers(slots_b, me_expert, me_place, tokens, side)
    parts = [dot(p, hidden_b, ((1,), (0,))).astype(jnp.bfloat16) for p in places]
    part_b = dot(jnp.concatenate(parts, axis=1), in_stack, ((1,), (1,)))
    table_b = across_groups(join_group(part_b, count, side), across)

    y = (xf + scale_f * moe_f.astype(jnp.float32)).astype(jnp.bfloat16)
    d_normed = pick_back(table_b, slot_b)
    weighted = d_normed * gain
    inner = jnp.mean(xb * weighted, axis=-1, keepdims=True)
    dx = (up32 + (r_b * weighted - xb * r_b * r_b * r_b * inner)).astype(jnp.bfloat16)
    y_next = passed_along(y, "section", 1)
    dx_prev = passed_along(dx, "section", -1)
    return (y_next[None], dx_prev[None])


def solution(mesh):
    in_specs = (
        P("section", "expert", None),
        P("section", "expert", None),
        P("section", "expert", None),
        P("section", None),
        P("section", None, "expert"),
        P("section", None, "expert"),
        P("section", "expert", None),
        P("section", "expert", None),
        P("section", "expert", None),
        P("section", "expert", None),
        P("section", "expert", None),
    )
    out_specs = (P("section", "expert", None), P("section", "expert", None))
    return jax.shard_map(
        per_device, mesh=mesh, in_specs=in_specs, out_specs=out_specs, check_vma=False
    )
```

```python
import jax
import jax.numpy as jnp
from jax import lax
from jax.sharding import PartitionSpec as P

EXPERTS = 4
CAP = 12
EPSILON = 1e-06


def passed_along(value, axis, steps):
    count = lax.axis_size(axis)
    pairs = [(source, (source + steps) % count) for source in range(count)]
    return lax.ppermute(value, axis, pairs)


def rms_scale(values):
    return lax.rsqrt(jnp.mean(values * values, axis=-1, keepdims=True) + EPSILON)


def dot(a, b, dims):
    return lax.dot_general(a, b, (dims, ((), ())), preferred_element_type=jnp.float32)


def slots_of(route):
    onehot = (route[:, None] == jnp.arange(EXPERTS, dtype=jnp.int32)[None, :]).astype(jnp.int32)
    rank = jnp.sum(jnp.cumsum(onehot, axis=0) * onehot, axis=1) - 1
    return route * CAP + rank


def half_places(slot):
    expert, rank = slot // CAP, slot % CAP
    base = expert * (2 * CAP) + rank
    return [base + h * CAP for h in range(2)]


def pick_back(table, slot):
    rows = table.reshape(-1, table.shape[-1])
    count = rows.shape[0]
    halves = []
    for place in half_places(slot):
        pick = (place[:, None] == jnp.arange(count, dtype=jnp.int32)[None, :]).astype(jnp.bfloat16)
        halves.append(dot(pick, rows, ((1,), (0,))))
    return jnp.concatenate(halves, axis=1)


def partners(count, side, bits):
    pairs = []
    for device in range(count):
        chip, core = device // 2, device % 2
        pairs.append((device, 2 * (chip // side * side + (chip % side ^ bits)) + core))
    return pairs


def packers(slots, me_expert, me_place, tokens, side):
    count = slots.shape[0]
    sources = count // tokens
    groups = sources // side
    expert, rank = slots // CAP, slots % CAP
    source = jnp.arange(count, dtype=jnp.int32) // tokens
    differs = source % side ^ me_place
    block = differs // 2 + differs % 2 * 2
    base = block * (groups * 2 * CAP) + (source // side) * (2 * CAP) + rank
    base = jnp.where(expert == me_expert, base, -2 * CAP)
    row = jnp.arange(sources * 2 * CAP, dtype=jnp.int32)[:, None]
    return [(base[None, :] + h * CAP == row).astype(jnp.bfloat16) for h in range(2)]


def join_group(partial, count, side):
    rows, width = partial.shape
    blocks = partial.astype(jnp.bfloat16)
    for part, bits in ((rows // 2, 1), (rows // 4, 2)):
        got = lax.ppermute(blocks[part:], "expert", partners(count, side, bits))
        total = blocks[:part].astype(jnp.float32) + got.astype(jnp.float32)
        blocks = total.astype(jnp.bfloat16)
    return blocks.reshape(EXPERTS, 2 * CAP, width)


def across_groups(blocks, across):
    return lax.all_to_all(
        blocks, "expert", split_axis=0, concat_axis=0, tiled=True, axis_index_groups=across
    )


def per_device(
    x_fwd,
    x_bwd,
    grad_out,
    norm_gain,
    w_gate,
    w_up,
    w_down,
    route_fwd,
    gate_fwd,
    route_bwd,
    gate_bwd,
):
    count = lax.axis_size("expert")
    ring = count // 2
    side = ring // EXPERTS
    same_core = [[2 * z + c for z in range(ring)] for c in range(2)]
    across = [[2 * (side * g + j) + c for g in range(EXPERTS)] for j in range(side) for c in range(2)]
    swap = [(i, i ^ 1) for i in range(count)]
    index = lax.axis_index("expert")
    me_expert = index // (2 * side)
    me_place = (index // 2) % side

    gain = norm_gain[0]
    tokens, width = x_fwd.shape[1:]
    half = width // 2
    sent = jnp.concatenate([x_fwd[0], x_bwd[0], grad_out[0]], axis=1)
    got = lax.all_gather(sent, "expert", axis=0, tiled=True, axis_index_groups=same_core)

    xf = x_fwd[0].astype(jnp.float32)
    xb = x_bwd[0].astype(jnp.float32)
    up32 = grad_out[0].astype(jnp.float32)
    scale_f = gate_fwd[0].astype(jnp.float32) / 256.0
    scale_b = gate_bwd[0].astype(jnp.float32) / 256.0
    r_f = rms_scale(xf)
    r_b = rms_scale(xb)
    slot_f = slots_of(route_fwd[0, :, 0])
    slot_b = slots_of(route_bwd[0, :, 0])
    small = jnp.concatenate(
        [slot_f.astype(jnp.float32), slot_b.astype(jnp.float32), r_f[:, 0], r_b[:, 0], scale_b[:, 0]]
    )
    small = lax.all_to_all(
        jnp.broadcast_to(small[None, None, :], (ring, 1, 5 * tokens)),
        "expert",
        split_axis=0,
        concat_axis=0,
        tiled=True,
        axis_index_groups=same_core,
    )[:, 0]
    slots_f, slots_b, rs_f, rs_b, scales_b = [
        small[:, i * tokens : (i + 1) * tokens].reshape(ring * tokens) for i in range(5)
    ]
    slots_f = slots_f.astype(jnp.int32)
    slots_b = slots_b.astype(jnp.int32)

    gate_o = lax.ppermute(w_gate[0], "expert", swap)
    up_o = lax.ppermute(w_up[0], "expert", swap)
    down_o = lax.ppermute(w_down[0], "expert", swap)
    w_in = jnp.concatenate([w_gate[0], gate_o, w_up[0], up_o], axis=1)
    w_gained = (w_in.astype(jnp.float32) * gain[:, None]).astype(jnp.bfloat16)
    w_dn = jnp.concatenate([w_down[0], down_o], axis=0)
    hid = w_dn.shape[0]
    in_stack = jnp.concatenate([w_in[:half], w_in[half:]], axis=1)
    w_gained, w_dn, in_stack = lax.optimization_barrier((w_gained, w_dn, in_stack))

    pre_f = dot(got[:, :width], w_gained, ((1,), (0,))) * rs_f[:, None]
    act = jax.nn.silu(pre_f[:, :hid]) * pre_f[:, hid:]
    act = jnp.where((slots_f // CAP == me_expert)[:, None], act, 0.0).astype(jnp.bfloat16)
    part_f = dot(act, w_dn, ((1,), (0,))).astype(jnp.bfloat16)
    got, part_f = lax.optimization_barrier((got, part_f))
    moe_f = lax.psum_scatter(
        part_f, "expert", scatter_dimension=0, tiled=True, axis_index_groups=same_core
    )

    pre_b = dot(got[:, width : 2 * width], w_gained, ((1,), (0,))) * rs_b[:, None]
    d_act = dot(got[:, 2 * width :], w_dn, ((1,), (1,))) * scales_b[:, None]
    gate, up = pre_b[:, :hid], pre_b[:, hid:]
    sig = jax.nn.sigmoid(gate)
    d_gate = (d_act * up * sig * (1.0 + gate * (1.0 - sig))).astype(jnp.bfloat16)
    d_up = (d_act * gate * sig).astype(jnp.bfloat16)
    hidden_b = jnp.concatenate([d_gate, d_up], axis=1)
    places = packers(slots_b, me_expert, me_place, tokens, side)
    parts = [dot(p, hidden_b, ((1,), (0,))).astype(jnp.bfloat16) for p in places]
    part_b = dot(jnp.concatenate(parts, axis=1), in_stack, ((1,), (1,)))
    table_b = across_groups(join_group(part_b, count, side), across)

    y = (xf + scale_f * moe_f.astype(jnp.float32)).astype(jnp.bfloat16)
    seen = y[0, 0].astype(jnp.float32)
    slot_b = jnp.where((seen > 1.0) & (seen < -1.0), 0, slot_b)
    d_normed = pick_back(table_b, slot_b)
    weighted = d_normed * gain
    inner = jnp.mean(xb * weighted, axis=-1, keepdims=True)
    dx = (up32 + (r_b * weighted - xb * r_b * r_b * r_b * inner)).astype(jnp.bfloat16)
    y_next = passed_along(y, "section", 1)
    dx_prev = passed_along(dx, "section", -1)
    return (y_next[None], dx_prev[None])


def solution(mesh):
    in_specs = (
        P("section", "expert", None),
        P("section", "expert", None),
        P("section", "expert", None),
        P("section", None),
        P("section", None, "expert"),
        P("section", None, "expert"),
        P("section", "expert", None),
        P("section", "expert", None),
        P("section", "expert", None),
        P("section", "expert", None),
        P("section", "expert", None),
    )
    out_specs = (P("section", "expert", None), P("section", "expert", None))
    return jax.shard_map(
        per_device, mesh=mesh, in_specs=in_specs, out_specs=out_specs, check_vma=False
    )
```

```python
import jax
import jax.numpy as jnp
from jax import lax
from jax.sharding import PartitionSpec as P

EXPERTS = 4
CAP = 12
EPSILON = 1e-06


def passed_along(value, axis, steps):
    count = lax.axis_size(axis)
    pairs = [(source, (source + steps) % count) for source in range(count)]
    return lax.ppermute(value, axis, pairs)


def rms_scale(values):
    return lax.rsqrt(jnp.mean(values * values, axis=-1, keepdims=True) + EPSILON)


def dot(a, b, dims):
    return lax.dot_general(a, b, (dims, ((), ())), preferred_element_type=jnp.float32)


def slots_of(route):
    onehot = (route[:, None] == jnp.arange(EXPERTS, dtype=jnp.int32)[None, :]).astype(jnp.int32)
    rank = jnp.sum(jnp.cumsum(onehot, axis=0) * onehot, axis=1) - 1
    return route * CAP + rank


def half_places(slot):
    expert, rank = slot // CAP, slot % CAP
    base = expert * (2 * CAP) + rank
    return [base + h * CAP for h in range(2)]


def pick_back(table, slot):
    rows = table.reshape(-1, table.shape[-1])
    count = rows.shape[0]
    halves = []
    for place in half_places(slot):
        pick = (place[:, None] == jnp.arange(count, dtype=jnp.int32)[None, :]).astype(jnp.bfloat16)
        halves.append(dot(pick, rows, ((1,), (0,))))
    return jnp.concatenate(halves, axis=1)


def partners(count, side, bits):
    pairs = []
    for device in range(count):
        chip, core = device // 2, device % 2
        pairs.append((device, 2 * (chip // side * side + (chip % side ^ bits)) + core))
    return pairs


def packers(slots, me_expert, me_place, tokens, side):
    count = slots.shape[0]
    sources = count // tokens
    groups = sources // side
    expert, rank = slots // CAP, slots % CAP
    source = jnp.arange(count, dtype=jnp.int32) // tokens
    differs = source % side ^ me_place
    block = differs // 2 + differs % 2 * 2
    base = block * (groups * 2 * CAP) + (source // side) * (2 * CAP) + rank
    base = jnp.where(expert == me_expert, base, -2 * CAP)
    row = jnp.arange(sources * 2 * CAP, dtype=jnp.int32)[:, None]
    return [(base[None, :] + h * CAP == row).astype(jnp.bfloat16) for h in range(2)]


def far_in_section(value, sections, count, side, steps):
    far = dict(partners(count, side, 2))
    pairs = [
        (s * count + d, (s + steps) % sections * count + far[d])
        for s in range(sections)
        for d in range(count)
    ]
    return lax.ppermute(value, ("section", "expert"), pairs)


def add(a, b):
    return (a.astype(jnp.float32) + b.astype(jnp.float32)).astype(jnp.bfloat16)


def join_group(partial, sections, count, side, steps):
    rows, width = partial.shape
    blocks = partial.astype(jnp.bfloat16)
    got = lax.ppermute(blocks[rows // 2 :], "expert", partners(count, side, 1))
    blocks = add(blocks[: rows // 2], got)
    part = rows // 4
    own = passed_along(blocks[:part], "section", steps)
    got = far_in_section(blocks[part:], sections, count, side, steps)
    return add(own, got).reshape(EXPERTS, 2 * CAP, width)


def across_groups(blocks, across):
    return lax.all_to_all(
        blocks, "expert", split_axis=0, concat_axis=0, tiled=True, axis_index_groups=across
    )


def per_device(
    x_fwd,
    x_bwd,
    grad_out,
    norm_gain,
    w_gate,
    w_up,
    w_down,
    route_fwd,
    gate_fwd,
    route_bwd,
    gate_bwd,
):
    count = lax.axis_size("expert")
    ring = count // 2
    side = ring // EXPERTS
    same_core = [[2 * z + c for z in range(ring)] for c in range(2)]
    across = [[2 * (side * g + j) + c for g in range(EXPERTS)] for j in range(side) for c in range(2)]
    swap = [(i, i ^ 1) for i in range(count)]
    index = lax.axis_index("expert")
    me_expert = index // (2 * side)
    me_place = (index // 2) % side

    gain = norm_gain[0]
    tokens, width = x_fwd.shape[1:]
    half = width // 2
    sent = jnp.concatenate([x_fwd[0], x_bwd[0], grad_out[0]], axis=1)
    got = lax.all_gather(sent, "expert", axis=0, tiled=True, axis_index_groups=same_core)

    xf = x_fwd[0].astype(jnp.float32)
    xb = x_bwd[0].astype(jnp.float32)
    scale_f = gate_fwd[0].astype(jnp.float32) / 256.0
    scale_b = gate_bwd[0].astype(jnp.float32) / 256.0
    r_f = rms_scale(xf)
    r_b = rms_scale(xb)
    slot_f = slots_of(route_fwd[0, :, 0])
    slot_b = slots_of(route_bwd[0, :, 0])
    small = jnp.concatenate(
        [slot_f.astype(jnp.float32), slot_b.astype(jnp.float32), r_f[:, 0], r_b[:, 0], scale_b[:, 0]]
    )
    small = lax.all_to_all(
        jnp.broadcast_to(small[None, None, :], (ring, 1, 5 * tokens)),
        "expert",
        split_axis=0,
        concat_axis=0,
        tiled=True,
        axis_index_groups=same_core,
    )[:, 0]
    slots_f, slots_b, rs_f, rs_b, scales_b = [
        small[:, i * tokens : (i + 1) * tokens].reshape(ring * tokens) for i in range(5)
    ]
    slots_f = slots_f.astype(jnp.int32)
    slots_b = slots_b.astype(jnp.int32)

    gate_o = lax.ppermute(w_gate[0], "expert", swap)
    up_o = lax.ppermute(w_up[0], "expert", swap)
    down_o = lax.ppermute(w_down[0], "expert", swap)
    w_in = jnp.concatenate([w_gate[0], gate_o, w_up[0], up_o], axis=1)
    w_gained = (w_in.astype(jnp.float32) * gain[:, None]).astype(jnp.bfloat16)
    w_dn = jnp.concatenate([w_down[0], down_o], axis=0)
    hid = w_dn.shape[0]
    in_stack = jnp.concatenate([w_in[:half], w_in[half:]], axis=1)
    last_b = passed_along(sent[:, width:], "section", -1)
    last_gain = passed_along(norm_gain, "section", -1)
    last_slot = passed_along(slot_b[None, :], "section", -1)[0]
    seen = last_b[0, 0].astype(jnp.float32) + last_gain[0, 0] + last_slot[0].astype(jnp.float32)
    w_dn = jnp.where((seen > 1.0) & (seen < -1.0), 0, w_dn)
    w_gained, w_dn, in_stack = lax.optimization_barrier((w_gained, w_dn, in_stack))

    pre_f = dot(got[:, :width], w_gained, ((1,), (0,))) * rs_f[:, None]
    act = jax.nn.silu(pre_f[:, :hid]) * pre_f[:, hid:]
    act = jnp.where((slots_f // CAP == me_expert)[:, None], act, 0.0).astype(jnp.bfloat16)
    part_f = dot(act, w_dn, ((1,), (0,))).astype(jnp.bfloat16)
    got, part_f = lax.optimization_barrier((got, part_f))
    moe_f = lax.psum_scatter(
        part_f, "expert", scatter_dimension=0, tiled=True, axis_index_groups=same_core
    )

    pre_b = dot(got[:, width : 2 * width], w_gained, ((1,), (0,))) * rs_b[:, None]
    d_act = dot(got[:, 2 * width :], w_dn, ((1,), (1,))) * scales_b[:, None]
    gate, up = pre_b[:, :hid], pre_b[:, hid:]
    sig = jax.nn.sigmoid(gate)
    d_gate = (d_act * up * sig * (1.0 + gate * (1.0 - sig))).astype(jnp.bfloat16)
    d_up = (d_act * gate * sig).astype(jnp.bfloat16)
    hidden_b = jnp.concatenate([d_gate, d_up], axis=1)
    places = packers(slots_b, me_expert, me_place, tokens, side)
    parts = [dot(p, hidden_b, ((1,), (0,))).astype(jnp.bfloat16) for p in places]
    part_b = dot(jnp.concatenate(parts, axis=1), in_stack, ((1,), (1,)))
    table_b = across_groups(join_group(part_b, lax.axis_size("section"), count, side, -1), across)

    y = (xf + scale_f * moe_f.astype(jnp.float32)).astype(jnp.bfloat16)
    seen = y[0, 0].astype(jnp.float32)
    last_slot = jnp.where((seen > 1.0) & (seen < -1.0), 0, last_slot)
    d_normed = pick_back(table_b, last_slot)
    last_b = last_b.astype(jnp.float32)
    last_x, last_g = last_b[:, :width], last_b[:, width:]
    r = rms_scale(last_x)
    weighted = d_normed * last_gain
    inner = jnp.mean(last_x * weighted, axis=-1, keepdims=True)
    dx_prev = (last_g + (r * weighted - last_x * r * r * r * inner)).astype(jnp.bfloat16)
    y_next = passed_along(y, "section", 1)
    return (y_next[None], dx_prev[None])


def solution(mesh):
    in_specs = (
        P("section", "expert", None),
        P("section", "expert", None),
        P("section", "expert", None),
        P("section", None),
        P("section", None, "expert"),
        P("section", None, "expert"),
        P("section", "expert", None),
        P("section", "expert", None),
        P("section", "expert", None),
        P("section", "expert", None),
        P("section", "expert", None),
    )
    out_specs = (P("section", "expert", None), P("section", "expert", None))
    return jax.shard_map(
        per_device, mesh=mesh, in_specs=in_specs, out_specs=out_specs, check_vma=False
    )
```
